512 devices in a mesh: node: 64 (over y, z), col: 8 (over x, core).
Axes of the slice: x: 4, y: 8, z: 8, core: 2. Of those that a mesh axis runs over, the one named last changes fastest.
Arguments:
- x_t: bfloat16 [512, 32768], P('col', 'node'), may hold values from -6 to 6
- adj_tiles: bfloat16 [4096, 128, 128], P('node'), may hold values from -0.1875 to 0.1875
- tile_rows: int32 [4096], P('node'), may hold values from 0 to 3
- tile_cols: int32 [4096], P('node'), may hold values from 0 to 255, as said below
- tile_counts: int32 [64], P('node'), may hold values from 8 to 64, as said below
- w_first: bfloat16 [512, 512], P('col'), may hold values from -0.25 to 0.25
- b_first: float32 [512], P('col'), may hold values from -3 to 3
- w_second: bfloat16 [512, 512], P('col'), may hold values from -0.25 to 0.25
- b_second: float32 [512], P('col'), may hold values from -3 to 3
Outputs:
- out_t: float32 [512, 32768], P('col', 'node')
The draws below stay inside these ranges and needn't reach their ends.
Inputs may be any that keep to these rules, and one draw needn't show every extreme that they name: `tile_cols`: column blocks q * 4 to q * 4 + 3 belong to device q of node. Among the live tiles of one device, at most 2 distinct column blocks belong to any one device, and every device's first 2 tiles name 2 distinct blocks of one device. `tile_counts`: some device has all 64 slots live.
All inputs are finite; a program needn't handle non-finite values.
Results may differ from the reference program's by a relative error of at most 0.004.
Values may be sent and summed in bfloat16 or wider, within the bound.
A program may use at most 64 MiB of HBM per device.

```python
import jax
import jax.numpy as jnp
from jax import lax

F = 512
BLK = 128
RB = 4
TILES = 64
CAP = 2
NBLK = 256
NODES = 32768
TILE_SLOTS = 4096


def draw_tile_cols(key, part):
    peer_count = NBLK // RB
    key_peer = jax.random.fold_in(key, 11)
    key_block = jax.random.fold_in(key, 23)
    peer_scores = jax.random.randint(key_peer, (peer_count, peer_count), 0, 1 << 20) * peer_count + jnp.arange(peer_count)[None, :]
    peer_order = jnp.argsort(peer_scores, axis=1).astype(jnp.int32)
    block_scores = jax.random.randint(key_block, (peer_count, peer_count, RB), 0, 1 << 20) * RB + jnp.arange(RB)[None, None, :]
    allowed = jnp.argsort(block_scores, axis=2)[:, :, :CAP].astype(jnp.int32)
    index = jnp.arange(TILES)
    which = index // CAP % peer_count
    slot = index % CAP
    owner = peer_order[:, which]
    source = jnp.arange(peer_count)[:, None]
    block = allowed[source, owner, slot[None, :]]
    return (owner * RB + block).reshape(-1).astype(jnp.int32)


def draw_tile_counts(key, part):
    peer_count = NBLK // RB
    shifts = jax.random.randint(jax.random.fold_in(key, 5), (peer_count,), 0, 4)
    counts = TILES // jnp.left_shift(jnp.ones((peer_count,), jnp.int32), shifts.astype(jnp.int32))
    chosen = jax.random.randint(jax.random.fold_in(key, 9), (), 0, peer_count)
    counts = jnp.where(jnp.arange(peer_count) == chosen, TILES, counts)
    return counts.astype(jnp.int32)


def plant(values, key, smallest, top_value):
    extent = values.shape
    spot = [jax.random.randint(jax.random.fold_in(key, axis), (), 0, extent[axis]) for axis in range(len(extent))]
    values = values.at[tuple(spot)].set(smallest)
    longest = extent.index(max(extent))
    spot[longest] = (spot[longest] + 1) % extent[longest]
    return values.at[tuple(spot)].set(top_value)


def block_scale(own_key, extent, pieces, least, high):
    gain, own = 1.0, jax.random.fold_in(own_key, 6)
    for axis_at, shards_of in pieces:
        heights = jnp.exp(jax.random.uniform(jax.random.fold_in(own, axis_at), (shards_of,), jnp.float32, least / len(pieces), high / len(pieces)))
        gain = gain * jnp.repeat(heights, extent[axis_at] // shards_of).reshape([-1 if axis == axis_at else 1 for axis in range(len(extent))])
    return gain


def centred(rng, shape, spread, bound, cuts=(), held_as=jnp.bfloat16):
    level = block_scale(rng, shape, cuts, -0.22, 0.18) if cuts else 1.0
    values = jax.random.normal(rng, shape, jnp.float32) * spread * level
    return jnp.minimum(jnp.maximum(values, -bound), bound).astype(held_as)


def setup_inputs(seed: int = 0) -> dict:
    splits = jax.random.split(jax.random.key(seed), 10)
    return {
        "x_t": centred(splits[0], (F, NODES), 1.0, 6.0, ((0, 8), (1, 64))),
        "adj_tiles": centred(splits[1], (TILE_SLOTS, BLK, BLK), (BLK * TILES // (2 * RB)) ** -0.5, 0.1875, ((0, 64),)),
        "tile_rows": plant(jax.random.randint(splits[2], (TILE_SLOTS,), 0, RB), jax.random.fold_in(splits[2], 1), 0, RB - 1).astype(jnp.int32),
        "tile_cols": draw_tile_cols(jax.random.fold_in(splits[9], 71), 0),
        "tile_counts": draw_tile_counts(jax.random.fold_in(splits[9], 71), 0),
        "w_first": centred(splits[5], (F, F), F ** -0.5, 0.25, ((0, 8),)),
        "b_first": centred(splits[6], (F,), 0.5, 3.0, ((0, 8),), jnp.float32),
        "w_second": centred(splits[7], (F, F), F ** -0.5, 0.25, ((0, 8),)),
        "b_second": centred(splits[8], (F,), 0.5, 3.0, ((0, 8),), jnp.float32),
    }


def aggregate(feat_t, adj_tiles, tile_rows, tile_cols, tile_counts):
    peer_count = NBLK // RB
    blocks = feat_t.reshape(F, NBLK, BLK)
    tile_values = adj_tiles.reshape(peer_count, TILES, BLK, BLK)
    row_table = tile_rows.reshape(peer_count, TILES)
    col_table = tile_cols.reshape(peer_count, TILES)

    def one_part(packed):
        values_p, rows_p, cols_p, count_p = packed
        x_blocks = jnp.take(blocks, cols_p.astype(jnp.int32), axis=1).astype(jnp.float32)
        products = jnp.einsum("fnj,nij->fni", x_blocks, values_p.astype(jnp.float32), precision=lax.Precision.HIGHEST)
        is_live = jnp.arange(TILES, dtype=jnp.int32) < count_p
        selector = ((rows_p[:, None] == jnp.arange(RB, dtype=jnp.int32)[None, :]) & is_live[:, None]).astype(jnp.float32)
        summed = jnp.einsum("fni,nb->fbi", products, selector, precision=lax.Precision.HIGHEST)
        return summed.reshape(F, RB * BLK)

    result = lax.map(one_part, (tile_values, row_table, col_table, tile_counts))
    return jnp.transpose(result, (1, 0, 2)).reshape(F, NODES).astype(jnp.bfloat16)


def reference(x_t, adj_tiles, tile_rows, tile_cols, tile_counts, w_first, b_first, w_second, b_second):
    y_first = aggregate(x_t, adj_tiles, tile_rows, tile_cols, tile_counts)
    z_first = jnp.dot(w_first, y_first, preferred_element_type=jnp.float32) + b_first[:, None]
    h_first = jnp.maximum(z_first, 0.0).astype(jnp.bfloat16)
    y_second = aggregate(h_first, adj_tiles, tile_rows, tile_cols, tile_counts)
    return jnp.dot(w_second, y_second, preferred_element_type=jnp.float32) + b_second[:, None]
```

```python
import jax
import jax.numpy as jnp
from jax import lax
from jax.experimental import pallas as pl
from jax.experimental.pallas import tpu as pltpu
from jax.sharding import PartitionSpec as P

BLK = 128
RB = 4
GROUP = 8


def tile_sum(index_ref, rows_ref, live, gathered, tiles):
    feat = gathered.shape[1]
    total = tiles.shape[0]

    def step(g, acc):
        left, right = [], []
        for k in range(GROUP):
            t = g * GROUP + k
            block = gathered[index_ref[t]]
            row = jnp.where(t < live, rows_ref[t], RB)
            zero = jnp.zeros_like(block)
            left.append(jnp.concatenate([jnp.where(row == b, block, zero) for b in range(RB)], axis=0))
            right.append(tiles[t])
        return acc + lax.dot_general(
            jnp.concatenate(left, axis=1),
            jnp.concatenate(right, axis=1),
            (((1,), (1,)), ((), ())),
            preferred_element_type=jnp.float32,
        )

    return lax.fori_loop(0, total // GROUP, step, jnp.zeros((RB * feat, BLK), jnp.float32))


def agg_kernel(cols_ref, rows_ref, count_ref, g_ref, tiles_ref, bias_ref, out_ref):
    feat = g_ref.shape[1]
    acc = tile_sum(cols_ref, rows_ref, count_ref[0], g_ref, tiles_ref)
    for b in range(RB):
        out_ref[:, b * BLK : (b + 1) * BLK] = (acc[b * feat : (b + 1) * feat] + bias_ref[...]).astype(out_ref.dtype)


def aggregate(blocks, tiles, cols, rows, count, bias, dtype):
    feat = blocks.shape[1]
    gathered = lax.all_gather(blocks, "node", axis=0, tiled=True)
    smem = pl.BlockSpec(memory_space=pltpu.SMEM)
    vmem = pl.BlockSpec(memory_space=pltpu.VMEM)
    return pl.pallas_call(
        agg_kernel,
        out_shape=jax.ShapeDtypeStruct((feat, RB * BLK), dtype),
        in_specs=[smem, smem, smem, vmem, vmem, vmem],
        out_specs=vmem,
    )(cols, rows, count, gathered, tiles, bias)


def to_blocks(feat_t):
    feat = feat_t.shape[0]
    return jnp.transpose(feat_t.reshape(feat, RB, BLK), (1, 0, 2))


def body(x_t, adj_tiles, tile_rows, tile_cols, tile_counts, w_first, b_first, w_second, b_second):
    feat = x_t.shape[0]
    w_all = lax.all_gather(w_first, "col", axis=0, tiled=True)
    b_all = lax.all_gather(b_first, "col", axis=0, tiled=True)
    none = jnp.zeros((feat, 1), jnp.float32)
    y_first = aggregate(to_blocks(x_t), adj_tiles, tile_cols, tile_rows, tile_counts, none, jnp.bfloat16)
    y_all = lax.all_gather(y_first, "col", axis=0, tiled=True)
    z_first = jnp.dot(w_all, y_all, preferred_element_type=jnp.float32) + b_all[:, None]
    h_first = jnp.maximum(z_first, 0.0).astype(jnp.bfloat16)
    z_second = jnp.dot(w_second, h_first, preferred_element_type=jnp.float32).astype(jnp.bfloat16)
    return aggregate(to_blocks(z_second), adj_tiles, tile_cols, tile_rows, tile_counts, b_second[:, None], jnp.float32)


def solution(mesh):
    return jax.shard_map(
        body,
        mesh=mesh,
        in_specs=(
            P("col", "node"),
            P("node", None, None),
            P("node"),
            P("node"),
            P("node"),
            P("col", None),
            P("col"),
            P("col", None),
            P("col"),
        ),
        out_specs=P("col", "node"),
        check_vma=False,
    )
```

```python
import heapq
import itertools

import jax
import jax.numpy as jnp
from jax import lax
from jax.experimental import pallas as pl
from jax.experimental.pallas import tpu as pltpu
from jax.sharding import PartitionSpec as P

MESH = pl.DeviceIdType.MESH
BLK = 128
RB = 4
GROUP = 8
SIDE = 8
FAR, NEAR = 4, 3
HALF = 2
SLOTS = 64


def children(flow, at):
    first, second = (0, 1) if flow == 0 else (1, 0)
    out = []

    def step(axis):
        here = at[axis]
        for sign in (1, -1):
            if (sign > 0 and 0 <= here < FAR) or (sign < 0 and -NEAR < here <= 0):
                there = list(at)
                there[axis] += sign
                out.append((tuple(there), axis, sign))

    if at[second] == 0:
        step(first)
    step(second)
    return out


def depth(flow, at):
    return max([1 + depth(flow, there) for there, _, _ in children(flow, at)], default=0)


def arrival_order():
    wire, hop = 0.7, 1.7
    free = {}
    tick = itertools.count()
    events = [(0.0, next(tick), flow, (0, 0)) for flow in (0, 1)]
    order = []
    while events:
        now, _, flow, at = heapq.heappop(events)
        order.append((flow, at))
        for there, axis, sign in sorted(children(flow, at), key=lambda c: -depth(flow, c[0])):
            start = max(now, free.get((axis, sign), 0.0))
            free[(axis, sign)] = start + wire
            heapq.heappush(events, (free[(axis, sign)] + hop, next(tick), flow, there))
    return order


def slot_of(at):
    return (at[0] + NEAR) * SIDE + at[1] + NEAR


class Place:
    def __init__(self):
        self.node, self.col = lax.axis_index("node"), lax.axis_index("col")
        self.y, self.z = self.node // SIDE, self.node % SIDE
        self.x, self.core = self.col // 2, self.col % 2
        self.sign = 1 - 2 * self.core
        self.ys = {a: (self.y - self.sign * a + 2 * SIDE) % SIDE for a in range(-NEAR, FAR + 1)}
        self.zs = {a: (self.z - self.sign * a + 2 * SIDE) % SIDE for a in range(-NEAR, FAR + 1)}

    def source(self, at):
        return self.ys[at[0]] * SIDE + self.zs[at[1]]

    def toward(self, axis, sign):
        y, z = (self.ys[-sign], self.z) if axis == 0 else (self.y, self.zs[-sign])
        return (y * SIDE + z, self.col)

    def beside(self, dx, other):
        core = 1 - self.core if other else self.core
        return (self.node, (self.x + dx) % 4 * 2 + core)


def remote(src, dst, send, recv, device):
    return pltpu.make_async_remote_copy(
        src_ref=src, dst_ref=dst, send_sem=send, recv_sem=recv, device_id=device, device_id_type=MESH
    )


def node_gather(place, held, send, recv, ends, own, between=None):
    here = (place.node, place.col)
    last = 0
    for count, (flow, at) in enumerate(arrival_order()):
        rows = held.at[pl.ds(place.source(at) * RB + flow * HALF, HALF)]
        onward = sorted(children(flow, at), key=lambda c: -depth(flow, c[0]))
        if at != (0, 0):
            if not onward:
                last += 1
                continue
            remote(rows, rows, send, recv.at[flow * SLOTS + slot_of(at)], here).wait_recv()
        for there, axis, sign in onward:
            ending = not children(flow, there)
            sem = ends if ending else recv.at[flow * SLOTS + slot_of(there)]
            device = place.toward(axis, sign)
            if at == (0, 0) and own is not None:
                for k in range(flow * HALF, flow * HALF + HALF):
                    remote(own(k), held.at[place.node * RB + k], send, sem, device).start()
            else:
                remote(rows, rows, send, sem, device).start()
        if between is not None:
            between(count)
    whole = held.at[pl.ds(0, last * HALF)]
    remote(whole, whole, send, ends, here).wait_recv()
    sent = held.at[pl.ds(0, (SIDE * SIDE - 1) * RB)]
    remote(sent, sent, send, ends, here).wait_send()


class ColGather:
    def __init__(self, place, own, rows, feat, send, recv):
        self.place, self.own, self.rows, self.feat, self.send, self.recv = place, own, rows, feat, send, recv
        self.half = feat // 2

    def cut(self, x, core, part):
        start = (x % 4 * 2 + core) * self.feat
        if part is None:
            return self.rows.at[pl.ds(start, self.feat)]
        return self.rows.at[pl.ds(start + part * self.half, self.half)]

    def mine(self, part):
        if part is None:
            return self.own
        return self.own.at[pl.ds(part * self.half, self.half)]

    def begin(self):
        p = self.place
        for dx, part, sem in ((1, 0, 0), (-1, 1, 3), (1, 1, 1), (-1, 0, 2)):
            remote(self.mine(part), self.cut(p.x, p.core, part), self.send, self.recv.at[sem], p.beside(dx + 4, False)).start()
        remote(self.mine(None), self.cut(p.x, p.core, None), self.send, self.recv.at[4], p.beside(0, True)).start()

    def wait(self, dx, other, part, sem):
        p = self.place
        core = 1 - p.core if other else p.core
        rows = self.cut(p.x + dx + 4, core, part)
        remote(rows, rows, self.send, self.recv.at[sem], (p.node, p.col)).wait_recv()
        return rows

    def forward(self, stage):
        p = self.place
        if stage == 0:
            for dx, part, sem, on, far in ((-1, 0, 0, 1, 5), (1, 1, 3, -1, 6), (-1, 1, 1, 0, 0), (1, 0, 2, 0, 0)):
                rows = self.wait(dx, False, part, sem)
                if on:
                    remote(rows, rows, self.send, self.recv.at[far], p.beside(on + 4, False)).start()
                remote(rows, rows, self.send, self.recv.at[7 + sem], p.beside(0, True)).start()
        else:
            for part, sem in ((0, 5), (1, 6)):
                rows = self.wait(2, False, part, sem)
                remote(rows, rows, self.send, self.recv.at[6 + sem], p.beside(0, True)).start()

    def finish(self):
        self.wait(0, True, None, 4)
        for dx, part, sem in ((-1, 0, 7), (-1, 1, 8), (1, 0, 9), (1, 1, 10), (2, 0, 11), (2, 1, 12)):
            self.wait(dx, True, part, sem)
        sent = self.rows.at[pl.ds(0, 7 * self.feat)]
        remote(sent, sent, self.send, self.recv.at[0], (self.place.node, self.place.col)).wait_send()


def tile_sum(index_ref, rows_ref, live, gathered, tiles):
    feat = gathered.shape[1]
    total = tiles.shape[0]

    def step(g, acc):
        left, right = [], []
        for k in range(GROUP):
            t = g * GROUP + k
            block = gathered[index_ref[t]]
            row = jnp.where(t < live, rows_ref[t], RB)
            zero = jnp.zeros_like(block)
            left.append(jnp.concatenate([jnp.where(row == b, block, zero) for b in range(RB)], axis=0))
            right.append(tiles[t])
        return acc + lax.dot_general(
            jnp.concatenate(left, axis=1),
            jnp.concatenate(right, axis=1),
            (((1,), (1,)), ((), ())),
            preferred_element_type=jnp.float32,
        )

    return lax.fori_loop(0, total // GROUP, step, jnp.zeros((RB * feat, BLK), jnp.float32))


def as_column(row):
    size = row.shape[1]
    square = jnp.broadcast_to(row, (size, size))
    same = lax.broadcasted_iota(jnp.int32, (size, size), 0) == lax.broadcasted_iota(jnp.int32, (size, size), 1)
    return jnp.sum(jnp.where(same, square, 0.0), axis=1, keepdims=True)


def kernel(
    cols_ref, rows_ref, count_ref, x_ref, adj_ref, w1_ref, b1_ref, w2_ref, b2_ref, out_ref,
    held1, held2, tiles, w1_all, w2, b1_own, b1_all, y_own, y_all,
    recv1, recv2, col_recv, bias_recv, sends, local,
):
    feat = y_own.shape[0]
    place = Place()
    fetch = [
        pltpu.make_async_copy(adj_ref, tiles, local.at[0]),
        pltpu.make_async_copy(w2_ref, w2, local.at[1]),
        pltpu.make_async_copy(w1_ref, w1_all.at[pl.ds(place.col * feat, feat)], local.at[2]),
    ]
    for k in range(RB):
        fetch.append(pltpu.make_async_copy(x_ref.at[:, pl.ds(k * BLK, BLK)], held1.at[place.node * RB + k], local.at[3 + k]))
    for copy in fetch:
        copy.start()

    b1_own[...] = jnp.broadcast_to(as_column(b1_ref[...]), b1_own.shape)
    b1_all[pl.ds(place.col * feat, feat)] = b1_own[...]

    barrier = pltpu.get_barrier_semaphore()
    greeted = [place.toward(axis, sign) for axis in (0, 1) for sign in (1, -1)]
    greeted += [place.beside(dx, other) for dx in range(4) for other in (False, True) if dx or other]
    for device in greeted:
        pl.semaphore_signal(barrier, inc=1, device_id=device, device_id_type=MESH)
    pl.semaphore_wait(barrier, len(greeted))

    weights = ColGather(place, w1_ref, w1_all, feat, sends.at[2], col_recv.at[0])
    peers = [(dx, other) for dx in range(4) for other in (False, True) if dx or other]

    def bias_copy(index, dx, other, coming):
        core = 1 - place.core if other else place.core
        x = (place.x - dx + 4) % 4 if coming else place.x
        source = x * 2 + (core if coming else place.core)
        rows = b1_all.at[pl.ds(source * feat, feat)]
        return remote(b1_own, rows, sends.at[4], bias_recv.at[index], place.beside(dx, other))

    def between(count):
        if count == 1:
            weights.begin()
            for index, (dx, other) in enumerate(peers):
                bias_copy(index, dx, other, False).start()
        elif count == 20:
            weights.forward(0)
        elif count == 40:
            weights.forward(1)

    node_gather(place, held1, sends.at[0], recv1, recv1.at[2 * SLOTS], lambda k: x_ref.at[:, pl.ds(k * BLK, BLK)], between)
    weights.finish()
    for index, (dx, other) in enumerate(peers):
        bias_copy(index, dx, other, True).wait_recv()
    sent = b1_all.at[pl.ds(0, len(peers) * feat)]
    remote(sent, sent, sends.at[4], bias_recv.at[0], (place.node, place.col)).wait_send()
    for copy in fetch:
        copy.wait()

    live = count_ref[0]
    acc = tile_sum(cols_ref, rows_ref, live, held1, tiles)
    for b in range(RB):
        y_own[:, b * BLK : (b + 1) * BLK] = acc[b * feat : (b + 1) * feat].astype(y_own.dtype)
    y_all[pl.ds(place.col * feat, feat)] = y_own[...]
    exchange = ColGather(place, y_own, y_all, feat, sends.at[3], col_recv.at[1])
    exchange.begin()
    exchange.forward(0)
    exchange.forward(1)
    exchange.finish()

    wide = HALF * BLK
    step_rows = 128
    for n in range(RB // HALF):
        columns = pl.ds(n * wide, wide)
        total = jnp.zeros((feat, wide), jnp.float32)
        for m in range(w1_all.shape[0] // step_rows):
            span = pl.ds(m * step_rows, step_rows)
            z = jnp.dot(w1_all[span, :], y_all[:, columns], preferred_element_type=jnp.float32)
            bias = b1_all[span, :]
            h = jnp.maximum(z + jnp.concatenate([bias] * HALF, axis=1), 0.0).astype(jnp.bfloat16)
            total += jnp.dot(w2[:, span], h, preferred_element_type=jnp.float32)
        for k in range(HALF):
            held2[place.node * RB + n * HALF + k] = total[:, k * BLK : (k + 1) * BLK].astype(jnp.bfloat16)

    node_gather(place, held2, sends.at[1], recv2, recv2.at[2 * SLOTS], None)
    acc = tile_sum(cols_ref, rows_ref, live, held2, tiles)
    bias = as_column(b2_ref[...])
    for b in range(RB):
        out_ref[:, b * BLK : (b + 1) * BLK] = acc[b * feat : (b + 1) * feat] + bias


def body(x_t, adj_tiles, tile_rows, tile_cols, tile_counts, w_first, b_first, w_second, b_second):
    feat, nodes = x_t.shape
    channels = w_first.shape[1]
    blocks = SIDE * SIDE * RB
    smem = pl.BlockSpec(memory_space=pltpu.SMEM)
    vmem = pl.BlockSpec(memory_space=pltpu.VMEM)
    hbm = pl.BlockSpec(memory_space=pl.ANY)
    dma = pltpu.SemaphoreType.DMA
    bf16 = jnp.bfloat16
    return pl.pallas_call(
        kernel,
        out_shape=jax.ShapeDtypeStruct((feat, nodes), jnp.float32),
        in_specs=[smem, smem, smem, hbm, hbm, hbm, vmem, hbm, vmem],
        out_specs=vmem,
        scratch_shapes=[
            pltpu.VMEM((blocks, feat, BLK), bf16),
            pltpu.VMEM((blocks, feat, BLK), bf16),
            pltpu.VMEM(adj_tiles.shape, bf16),
            pltpu.VMEM((channels, channels), bf16),
            pltpu.VMEM((feat, channels), bf16),
            pltpu.VMEM((feat, BLK), jnp.float32),
            pltpu.VMEM((channels, BLK), jnp.float32),
            pltpu.VMEM((feat, nodes), bf16),
            pltpu.VMEM((channels, nodes), bf16),
            dma((2 * SLOTS + 1,)),
            dma((2 * SLOTS + 1,)),
            dma((2, 13)),
            dma((7,)),
            dma((5,)),
            dma((7,)),
        ],
        compiler_params=pltpu.CompilerParams(collective_id=0, has_side_effects=True),
    )(tile_cols, tile_rows, tile_counts, x_t, adj_tiles, w_first, b_first[None, :], w_second, b_second[None, :])


def solution(mesh):
    return jax.shard_map(
        body,
        mesh=mesh,
        in_specs=(
            P("col", "node"),
            P("node", None, None),
            P("node"),
            P("node"),
            P("node"),
            P("col", None),
            P("col"),
            P("col", None),
            P("col"),
        ),
        out_specs=P("col", "node"),
        check_vma=False,
    )
```

```python
import heapq
import itertools

import jax
import jax.numpy as jnp
from jax import lax
from jax.experimental import pallas as pl
from jax.experimental.pallas import tpu as pltpu
from jax.sharding import PartitionSpec as P

MESH = pl.DeviceIdType.MESH
BLK = 128
RB = 4
GROUP = 8
SIDE = 8
FAR, NEAR = 4, 3
HALF = 2
CAP = 2
WIRE, BASE, HOP = 1.0, 0.9, 0.8
SLOTS = 64


SPINES = (0, 3, -3)
BESIDE = {0: (1, -1), 3: (1, -1), -3: (1,)}


def onward(at):
    a, b = at
    out = [(d, 0) for d in SPINES if d] if at == (0, 0) else []
    if 0 <= b < FAR:
        out.append((a, b + 1))
    if -NEAR < b <= 0:
        out.append((a, b - 1))
    return out


def arrival_order():
    wire, base, hop = WIRE, BASE, HOP
    free = {}
    tick = itertools.count()
    events = [(0.0, next(tick), (0, 0))]
    order = []
    while events:
        now, _, at = heapq.heappop(events)
        order.append(at)
        for there in onward(at):
            da, db = there[0] - at[0], there[1] - at[1]
            link = (da != 0, da + db > 0)
            start = max(now, free.get(link, 0.0))
            free[link] = start + wire * abs(da + db)
            heapq.heappush(events, (start + wire + base + hop * abs(da + db), next(tick), there))
    return order


def slot_of(at):
    return (at[0] + NEAR) * SIDE + at[1] + NEAR


class Place:
    def __init__(self):
        self.node, self.col = lax.axis_index("node"), lax.axis_index("col")
        y, z = self.node // SIDE, self.node % SIDE
        self.x, self.core = self.col // 2, self.col % 2
        self.u, v = y + (z - y) * self.core, z + (y - z) * self.core
        across, along = SIDE - (SIDE - 1) * self.core, 1 + (SIDE - 1) * self.core
        steps = range(-FAR, FAR + 1)
        self.us = {a: (self.u + a + SIDE) % SIDE * across for a in steps}
        self.vs = {b: (v - b + SIDE) % SIDE * along for b in steps}

    def source(self, at):
        return self.us[at[0]] + self.vs[at[1]]

    def target(self, da, db):
        return (self.us[-da] + self.vs[-db], self.col)

    def beside(self, dx, other):
        core = 1 - self.core if other else self.core
        return (self.node, (self.x + dx) % 4 * 2 + core)


def remote(src, dst, send, recv, device):
    return pltpu.make_async_remote_copy(
        src_ref=src, dst_ref=dst, send_sem=send, recv_sem=recv, device_id=device, device_id_type=MESH
    )


def node_gather(place, held, stage, table, send, recv, ends, between=None):
    here = (place.node, place.col)
    picked, ready = 0, []

    def pick(at):
        nonlocal picked
        base = place.source(at) * RB
        blocks = [held[base + k] for k in range(RB)]
        copies = []
        for da in BESIDE[at[0]]:
            for lane in range(CAP):
                want = table[(1 - da) // 2, place.source(at), lane]
                block = blocks[RB - 1]
                for k in range(RB - 1):
                    block = jnp.where(want == k, blocks[k], block)
                stage[picked, lane] = block
            pair = held.at[pl.ds(base, CAP)]
            copies.append(remote(stage.at[picked], pair, send, ends, place.target(da, 0)))
            picked += 1
        return copies

    order = arrival_order()
    for count, at in enumerate(order):
        rows = held.at[pl.ds(place.source(at) * RB, RB)]
        if at != (0, 0):
            remote(rows, rows, send, recv.at[slot_of(at)], here).wait_recv()
        for there in onward(at):
            remote(rows, rows, send, recv.at[slot_of(there)], place.target(there[0] - at[0], there[1] - at[1])).start()
        if between is not None:
            between(count)
        for copy in ready:
            copy.start()
        ready = pick(order[count - 1]) if count else []
    for copy in ready:
        copy.start()
    for copy in pick(order[-1]):
        copy.start()
    came = held.at[pl.ds(0, picked * CAP)]
    remote(came, came, send, ends, here).wait_recv()
    sent = held.at[pl.ds(0, (len(order) - 1) * RB + picked * CAP)]
    remote(sent, sent, send, ends, here).wait_send()


class ColGather:
    def __init__(self, place, own, rows, feat, send, recv):
        self.place, self.own, self.rows, self.feat, self.send, self.recv = place, own, rows, feat, send, recv
        self.half = feat // 2

    def cut(self, x, core, part):
        start = (x % 4 * 2 + core) * self.feat
        if part is None:
            return self.rows.at[pl.ds(start, self.feat)]
        return self.rows.at[pl.ds(start + part * self.half, self.half)]

    def mine(self, part):
        if part is None:
            return self.own
        return self.own.at[pl.ds(part * self.half, self.half)]

    def begin(self):
        p = self.place
        for dx, part, sem in ((1, 0, 0), (-1, 1, 3), (1, 1, 1), (-1, 0, 2)):
            remote(self.mine(part), self.cut(p.x, p.core, part), self.send, self.recv.at[sem], p.beside(dx + 4, False)).start()
        remote(self.mine(None), self.cut(p.x, p.core, None), self.send, self.recv.at[4], p.beside(0, True)).start()

    def wait(self, dx, other, part, sem):
        p = self.place
        core = 1 - p.core if other else p.core
        rows = self.cut(p.x + dx + 4, core, part)
        remote(rows, rows, self.send, self.recv.at[sem], (p.node, p.col)).wait_recv()
        return rows

    def forward(self, stage):
        p = self.place
        if stage == 0:
            for dx, part, sem, on, far in ((-1, 0, 0, 1, 5), (1, 1, 3, -1, 6), (-1, 1, 1, 0, 0), (1, 0, 2, 0, 0)):
                rows = self.wait(dx, False, part, sem)
                if on:
                    remote(rows, rows, self.send, self.recv.at[far], p.beside(on + 4, False)).start()
                remote(rows, rows, self.send, self.recv.at[7 + sem], p.beside(0, True)).start()
        else:
            for part, sem in ((0, 5), (1, 6)):
                rows = self.wait(2, False, part, sem)
                remote(rows, rows, self.send, self.recv.at[6 + sem], p.beside(0, True)).start()

    def finish(self):
        self.wait(0, True, None, 4)
        for dx, part, sem in ((-1, 0, 7), (-1, 1, 8), (1, 0, 9), (1, 1, 10), (2, 0, 11), (2, 1, 12)):
            self.wait(dx, True, part, sem)
        sent = self.rows.at[pl.ds(0, 7 * self.feat)]
        remote(sent, sent, self.send, self.recv.at[0], (self.place.node, self.place.col)).wait_send()


def tile_sum(index_ref, rows_ref, live, gathered, tiles):
    feat = gathered.shape[1]
    total = tiles.shape[0]

    def step(g, acc):
        left, right = [], []
        for k in range(GROUP):
            t = g * GROUP + k
            block = gathered[index_ref[0, t]]
            row = jnp.where(t < live, rows_ref[t], RB)
            zero = jnp.zeros_like(block)
            left.append(jnp.concatenate([jnp.where(row == b, block, zero) for b in range(RB)], axis=0))
            right.append(tiles[t])
        return acc + lax.dot_general(
            jnp.concatenate(left, axis=1),
            jnp.concatenate(right, axis=1),
            (((1,), (1,)), ((), ())),
            preferred_element_type=jnp.float32,
        )

    return lax.fori_loop(0, total // GROUP, step, jnp.zeros((RB * feat, BLK), jnp.float32))


def as_column(row):
    size = row.shape[1]
    square = jnp.broadcast_to(row, (size, size))
    same = lax.broadcasted_iota(jnp.int32, (size, size), 0) == lax.broadcasted_iota(jnp.int32, (size, size), 1)
    return jnp.sum(jnp.where(same, square, 0.0), axis=1, keepdims=True)


def tile_plan(place, cols, live):
    total, nodes = cols.shape[1], SIDE * SIDE
    node, block = cols >> 2, cols & (RB - 1)
    alive = lax.broadcasted_iota(jnp.int32, (1, total), 1) < live
    node = jnp.where(alive, node, nodes)
    hit = lax.broadcasted_iota(jnp.int32, (nodes, total), 0) == node
    first = jnp.min(jnp.where(hit, block, RB - 1).astype(jnp.float32), axis=1, keepdims=True).astype(jnp.int32)
    last = jnp.max(jnp.where(hit, block, 0).astype(jnp.float32), axis=1, keepdims=True).astype(jnp.int32)
    lowest = jnp.min(jnp.where(hit, first, RB - 1).astype(jnp.float32), axis=0, keepdims=True).astype(jnp.int32)
    owner = cols >> 2
    u = (owner >> 3) * (1 - place.core) + (owner & (SIDE - 1)) * place.core
    a = (u - place.u + SIDE) & (SIDE - 1)
    line = (a == 0) | (a == 3) | (a == SIDE - 3)
    slot = jnp.where(line, block, jnp.where(block == lowest, 0, 1))
    return first, last, owner * RB + slot


def kernel(
    colrow_ref, rows_ref, count_ref, x_ref, adj_ref, w1_ref, b1_ref, w2_ref, b2_ref, out_ref,
    held1, held2, tiles, w1_all, w2, b1_own, b1_all, y_own, y_all,
    stage, wanted, wanted_by, index_row, table, index_ref,
    recv1, recv2, col_recv, bias_recv, want_recv, sends, local,
):
    feat = y_own.shape[0]
    place = Place()
    fetch = [
        pltpu.make_async_copy(adj_ref, tiles, local.at[0]),
        pltpu.make_async_copy(w2_ref, w2, local.at[1]),
        pltpu.make_async_copy(w1_ref, w1_all.at[pl.ds(place.col * feat, feat)], local.at[2]),
    ]
    for k in range(RB):
        fetch.append(pltpu.make_async_copy(x_ref.at[:, pl.ds(k * BLK, BLK)], held1.at[place.node * RB + k], local.at[3 + k]))
    for copy in fetch:
        copy.start()

    b1_own[...] = jnp.broadcast_to(as_column(b1_ref[...]), b1_own.shape)
    b1_all[pl.ds(place.col * feat, feat)] = b1_own[...]
    first, last, index = tile_plan(place, colrow_ref[...], count_ref[0])
    lane = lax.broadcasted_iota(jnp.int32, wanted.shape, 1)
    wanted[...] = jnp.where(lane == 0, first, last)
    index_row[:, 0 : index.shape[1]] = jnp.broadcast_to(index, (8, index.shape[1]))
    for copy in fetch[3:]:
        copy.wait()

    barrier = pltpu.get_barrier_semaphore()
    greeted = [place.target(d, 0) for d in (1, -1, 3, -3)] + [place.target(0, d) for d in (1, -1)]
    greeted += [place.beside(dx, other) for dx in range(4) for other in (False, True) if dx or other]
    for device in greeted:
        pl.semaphore_signal(barrier, inc=1, device_id=device, device_id_type=MESH)
    pl.semaphore_wait(barrier, len(greeted))

    asked = [remote(wanted, wanted_by.at[i], sends.at[5 + i], want_recv.at[i], place.target(d, 0)) for i, d in ((1, 1), (0, -1))]
    for copy in asked:
        copy.start()
    to_index = pltpu.make_async_copy(index_row, index_ref, local.at[7])
    to_index.start()
    to_table = pltpu.make_async_copy(wanted_by, table, local.at[8])

    weights = ColGather(place, w1_ref, w1_all, feat, sends.at[2], col_recv.at[0])
    peers = [(dx, other) for dx in range(4) for other in (False, True) if dx or other]

    def bias_copy(index, dx, other, coming):
        core = 1 - place.core if other else place.core
        x = (place.x - dx + 4) % 4 if coming else place.x
        source = x * 2 + (core if coming else place.core)
        rows = b1_all.at[pl.ds(source * feat, feat)]
        return remote(b1_own, rows, sends.at[4], bias_recv.at[index], place.beside(dx, other))

    def between(count):
        if count == 1:
            for copy in asked:
                copy.wait()
            to_table.start()
            weights.begin()
            for index, (dx, other) in enumerate(peers):
                bias_copy(index, dx, other, False).start()
            to_table.wait()
        elif count == 8:
            weights.forward(0)
        elif count == 16:
            weights.forward(1)

    node_gather(place, held1, stage, table, sends.at[0], recv1, recv1.at[SLOTS], between)
    to_index.wait()
    weights.finish()
    for index, (dx, other) in enumerate(peers):
        bias_copy(index, dx, other, True).wait_recv()
    sent = b1_all.at[pl.ds(0, len(peers) * feat)]
    remote(sent, sent, sends.at[4], bias_recv.at[0], (place.node, place.col)).wait_send()
    for copy in fetch[:3]:
        copy.wait()

    live = count_ref[0]
    acc = tile_sum(index_ref, rows_ref, live, held1, tiles)
    for b in range(RB):
        y_own[:, b * BLK : (b + 1) * BLK] = acc[b * feat : (b + 1) * feat].astype(y_own.dtype)
    y_all[pl.ds(place.col * feat, feat)] = y_own[...]
    exchange = ColGather(place, y_own, y_all, feat, sends.at[3], col_recv.at[1])
    exchange.begin()
    exchange.forward(0)
    exchange.forward(1)
    exchange.finish()

    wide = HALF * BLK
    step_rows = 128
    for n in range(RB // HALF):
        columns = pl.ds(n * wide, wide)
        total = jnp.zeros((feat, wide), jnp.float32)
        for m in range(w1_all.shape[0] // step_rows):
            span = pl.ds(m * step_rows, step_rows)
            z = jnp.dot(w1_all[span, :], y_all[:, columns], preferred_element_type=jnp.float32)
            bias = b1_all[span, :]
            h = jnp.maximum(z + jnp.concatenate([bias] * HALF, axis=1), 0.0).astype(jnp.bfloat16)
            total += jnp.dot(w2[:, span], h, preferred_element_type=jnp.float32)
        for k in range(HALF):
            held2[place.node * RB + n * HALF + k] = total[:, k * BLK : (k + 1) * BLK].astype(jnp.bfloat16)

    node_gather(place, held2, stage, table, sends.at[1], recv2, recv2.at[SLOTS])
    acc = tile_sum(index_ref, rows_ref, live, held2, tiles)
    bias = as_column(b2_ref[...])
    for b in range(RB):
        out_ref[:, b * BLK : (b + 1) * BLK] = acc[b * feat : (b + 1) * feat] + bias


def body(x_t, adj_tiles, tile_rows, tile_cols, tile_counts, w_first, b_first, w_second, b_second):
    feat, nodes = x_t.shape
    channels = w_first.shape[1]
    blocks = SIDE * SIDE * RB
    smem = pl.BlockSpec(memory_space=pltpu.SMEM)
    vmem = pl.BlockSpec(memory_space=pltpu.VMEM)
    hbm = pl.BlockSpec(memory_space=pl.ANY)
    dma = pltpu.SemaphoreType.DMA
    bf16 = jnp.bfloat16
    return pl.pallas_call(
        kernel,
        out_shape=jax.ShapeDtypeStruct((feat, nodes), jnp.float32),
        in_specs=[vmem, smem, smem, hbm, hbm, hbm, vmem, hbm, vmem],
        out_specs=vmem,
        scratch_shapes=[
            pltpu.VMEM((blocks, feat, BLK), bf16),
            pltpu.VMEM((blocks, feat, BLK), bf16),
            pltpu.VMEM(adj_tiles.shape, bf16),
            pltpu.VMEM((channels, channels), bf16),
            pltpu.VMEM((feat, channels), bf16),
            pltpu.VMEM((feat, BLK), jnp.float32),
            pltpu.VMEM((channels, BLK), jnp.float32),
            pltpu.VMEM((feat, nodes), bf16),
            pltpu.VMEM((channels, nodes), bf16),
            pltpu.VMEM((5 * SIDE, CAP, feat, BLK), bf16),
            pltpu.VMEM((SIDE * SIDE, BLK), jnp.int32),
            pltpu.VMEM((2, SIDE * SIDE, BLK), jnp.int32),
            pltpu.VMEM((8, BLK), jnp.int32),
            pltpu.SMEM((2, SIDE * SIDE, BLK), jnp.int32),
            pltpu.SMEM((8, BLK), jnp.int32),
            dma((SLOTS + 1,)),
            dma((SLOTS + 1,)),
            dma((2, 13)),
            dma((7,)),
            dma((2,)),
            dma((7,)),
            dma((9,)),
        ],
        compiler_params=pltpu.CompilerParams(collective_id=0, has_side_effects=True),
    )(tile_cols[None, :], tile_rows, tile_counts, x_t, adj_tiles, w_first, b_first[None, :], w_second, b_second[None, :])


def solution(mesh):
    return jax.shard_map(
        body,
        mesh=mesh,
        in_specs=(
            P("col", "node"),
            P("node", None, None),
            P("node"),
            P("node"),
            P("node"),
            P("col", None),
            P("col"),
            P("col", None),
            P("col"),
        ),
        out_specs=P("col", "node"),
        check_vma=False,
    )
```

```python
import heapq
import itertools

import jax
import jax.numpy as jnp
from jax import lax
from jax.experimental import pallas as pl
from jax.experimental.pallas import tpu as pltpu
from jax.sharding import PartitionSpec as P

MESH = pl.DeviceIdType.MESH
BLK = 128
RB = 4
GROUP = 32
SIDE = 8
FAR, NEAR = 4, 3
HALF = 2
CAP = 2
WIRE, BASE, HOP = 0.6, 0.9, 0.5
TABLE = 2
SLOTS = 64


SPINES = (0, 3, -3)
BESIDE = {0: (1, -1), 3: (1, -1), -3: (1,)}
ROWS = (1, -1, 2, 4, -2)
SPANS = ((-1, 0), (1, 2), (-2, -2), (-3, -3), (3, 3), (4, 4))
FULL = SIDE * SIDE * RB


def onward(at):
    a, b = at
    out = []
    if 0 <= b < FAR:
        out.append((a, b + 1))
    if -NEAR < b <= 0:
        out.append((a, b - 1))
    return out + ([(d, 0) for d in SPINES if d] if at == (0, 0) else [])


def arrival_order():
    wire, base, hop = WIRE, BASE, HOP
    free = {}
    tick = itertools.count()
    events = [(0.0, next(tick), (0, 0))]
    order = []
    while events:
        now, _, at = heapq.heappop(events)
        order.append(at)
        for there in onward(at):
            da, db = there[0] - at[0], there[1] - at[1]
            link = (da != 0, da + db > 0)
            start = max(now, free.get(link, 0.0))
            free[link] = start + wire * abs(da + db)
            heapq.heappush(events, (start + wire + base + hop * abs(da + db), next(tick), there))
    return order


def slot_of(at):
    return (at[0] + NEAR) * SIDE + at[1] + NEAR


class Place:
    def __init__(self):
        self.node, self.col = lax.axis_index("node"), lax.axis_index("col")
        y, z = self.node // SIDE, self.node % SIDE
        self.x, self.core = self.col // 2, self.col % 2
        self.u, self.v = y + (z - y) * self.core, z + (y - z) * self.core
        across, along = SIDE - (SIDE - 1) * self.core, 1 + (SIDE - 1) * self.core
        steps = range(-FAR, FAR + 1)
        self.us = {a: (self.u + a + SIDE) % SIDE * across for a in steps}
        self.vs = {b: (self.v - b + SIDE) % SIDE * along for b in steps}

    def source(self, at):
        return self.us[at[0]] + self.vs[at[1]]

    def target(self, da, db):
        return (self.us[-da] + self.vs[-db], self.col)

    def beside(self, dx, other):
        core = 1 - self.core if other else self.core
        return (self.node, (self.x + dx) % 4 * 2 + core)


def remote(src, dst, send, recv, device):
    return pltpu.make_async_remote_copy(
        src_ref=src, dst_ref=dst, send_sem=send, recv_sem=recv, device_id=device, device_id_type=MESH
    )


def pair_at(a, b):
    return (ROWS.index(a) * SIDE + b + NEAR) * CAP


def node_gather(place, held, stage, table, send, recv, ends, start=1, between=None):
    here = (place.node, place.col)
    picked = set()
    waiting = []

    def pick(at):
        a, b = at
        base = place.source(at) * RB
        blocks = [held[base + k] for k in range(RB)]
        picked.add(at)
        copies = []
        low, high = next(span for span in SPANS if span[0] <= b <= span[1])
        for da in BESIDE[a]:
            for lane in range(CAP):
                want = table[(1 - da) // 2, place.source(at), lane]
                block = blocks[RB - 1]
                for k in range(RB - 1):
                    block = jnp.where(want == k, blocks[k], block)
                stage[pair_at(a + da, b) + lane] = block
            if all((a, other) in picked for other in range(low, high + 1)):
                first, size = pair_at(a + da, low), CAP * (high + 1 - low)
                pairs = held.at[pl.ds(FULL + first, size)]
                copies.append(remote(stage.at[pl.ds(first, size)], pairs, send, ends, place.target(da, 0)))
        return copies

    order = arrival_order()
    for count, at in enumerate(order):
        rows = held.at[pl.ds(place.source(at) * RB, RB)]
        if at != (0, 0):
            remote(rows, rows, send, recv.at[slot_of(at)], here).wait_recv()
        for there in onward(at):
            remote(rows, rows, send, recv.at[slot_of(there)], place.target(there[0] - at[0], there[1] - at[1])).start()
        if between is not None:
            between(count)
        if count >= start:
            for old in waiting + [at]:
                for copy in pick(old):
                    copy.start()
            waiting = []
        else:
            waiting.append(at)
    for at in waiting:
        for copy in pick(at):
            copy.start()
    came = held.at[pl.ds(0, len(ROWS) * SIDE * CAP)]
    remote(came, came, send, ends, here).wait_recv()
    sent = held.at[pl.ds(0, (len(order) - 1) * RB + len(ROWS) * SIDE * CAP)]
    remote(sent, sent, send, ends, here).wait_send()


class ColGather:
    def __init__(self, place, own, rows, feat, send, recv):
        self.place, self.own, self.rows, self.feat, self.send, self.recv = place, own, rows, feat, send, recv
        self.half = feat // 2

    def cut(self, x, core, part):
        start = (x % 4 * 2 + core) * self.feat
        if part is None:
            return self.rows.at[pl.ds(start, self.feat)]
        return self.rows.at[pl.ds(start + part * self.half, self.half)]

    def mine(self, part):
        if part is None:
            return self.own
        return self.own.at[pl.ds(part * self.half, self.half)]

    def begin(self):
        p = self.place
        for dx, sem in ((1, 0), (-1, 1), (2, 2)):
            remote(self.own, self.cut(p.x, p.core, None), self.send, self.recv.at[sem], p.beside(dx + 4, False)).start()
        remote(self.own, self.cut(p.x, p.core, None), self.send, self.recv.at[3], p.beside(0, True)).start()

    def wait(self, dx, other, sem):
        p = self.place
        core = 1 - p.core if other else p.core
        rows = self.cut(p.x + dx + 4, core, None)
        remote(rows, rows, self.send, self.recv.at[sem], (p.node, p.col)).wait_recv()
        return rows

    def forward(self, stage):
        p = self.place
        for dx, sem in ((-1, 0), (1, 1)) if stage == 0 else ((2, 2),):
            rows = self.wait(dx, False, sem)
            remote(rows, rows, self.send, self.recv.at[4 + sem], p.beside(0, True)).start()

    def finish(self):
        for dx, sem in ((0, 3), (-1, 4), (1, 5), (2, 6)):
            self.wait(dx, True, sem)
        sent = self.rows.at[pl.ds(0, 7 * self.feat)]
        remote(sent, sent, self.send, self.recv.at[0], (self.place.node, self.place.col)).wait_send()


def tile_sum(index_ref, rows_ref, live, gathered, tiles):
    feat = gathered.shape[1]
    total = tiles.shape[0]

    def step(g, acc):
        left, right = [], []
        for k in range(GROUP):
            t = g * GROUP + k
            block = gathered[index_ref[0, t]]
            row = jnp.where(t < live, rows_ref[t], RB)
            zero = jnp.zeros_like(block)
            left.append(jnp.concatenate([jnp.where(row == b, block, zero) for b in range(RB)], axis=0))
            right.append(tiles[t])
        return acc + lax.dot_general(
            jnp.concatenate(left, axis=1),
            jnp.concatenate(right, axis=1),
            (((1,), (1,)), ((), ())),
            preferred_element_type=jnp.float32,
        )

    return lax.fori_loop(0, total // GROUP, step, jnp.zeros((RB * feat, BLK), jnp.float32))


def as_column(row):
    size = row.shape[1]
    square = jnp.broadcast_to(row, (size, size))
    same = lax.broadcasted_iota(jnp.int32, (size, size), 0) == lax.broadcasted_iota(jnp.int32, (size, size), 1)
    return jnp.sum(jnp.where(same, square, 0.0), axis=1, keepdims=True)


def tile_plan(place, cols, live):
    total, nodes = cols.shape[1], SIDE * SIDE
    node, block = cols >> 2, cols & (RB - 1)
    alive = lax.broadcasted_iota(jnp.int32, (1, total), 1) < live
    node = jnp.where(alive, node, nodes)
    hit = lax.broadcasted_iota(jnp.int32, (nodes, total), 0) == node
    first = jnp.min(jnp.where(hit, block, RB - 1).astype(jnp.float32), axis=1, keepdims=True).astype(jnp.int32)
    last = jnp.max(jnp.where(hit, block, 0).astype(jnp.float32), axis=1, keepdims=True).astype(jnp.int32)
    lowest = jnp.min(jnp.where(hit, first, RB - 1).astype(jnp.float32), axis=0, keepdims=True).astype(jnp.int32)
    owner = cols >> 2
    u = (owner >> 3) * (1 - place.core) + (owner & (SIDE - 1)) * place.core
    a = (u - place.u + SIDE) & (SIDE - 1)
    line = (a == 0) | (a == 3) | (a == SIDE - 3)
    v = (owner & (SIDE - 1)) * (1 - place.core) + (owner >> 3) * place.core
    row = jnp.zeros_like(a)
    for i, at in enumerate(ROWS):
        row = jnp.where(a == at % SIDE, i, row)
    pair = (row * SIDE + ((place.v - v + NEAR) & (SIDE - 1))) * CAP
    beside = FULL + pair + jnp.where(block == lowest, 0, 1)
    return first, last, jnp.where(line, owner * RB + block, beside)


def kernel(
    colrow_ref, rows_ref, count_ref, x_ref, adj_ref, w1_ref, b1_ref, w2_ref, b2_ref, out_ref,
    held1, held2, tiles, w1_all, w2, b1_own, b1_all, y_own, y_all,
    stage, wanted, wanted_by, index_row, table, index_ref,
    recv1, recv2, col_recv, bias_recv, want_recv, sends, local,
):
    feat = y_own.shape[0]
    place = Place()
    fetch = [
        pltpu.make_async_copy(x_ref.at[:, pl.ds(k * BLK, BLK)], held1.at[place.node * RB + k], local.at[k]) for k in range(RB)
    ]
    fetch += [
        pltpu.make_async_copy(adj_ref, tiles, local.at[4]),
        pltpu.make_async_copy(w2_ref, w2, local.at[5]),
        pltpu.make_async_copy(w1_ref, w1_all.at[pl.ds(place.col * feat, feat)], local.at[6]),
    ]
    for copy in fetch:
        copy.start()

    barrier = pltpu.get_barrier_semaphore()
    greeted = [place.target(d, 0) for d in (1, -1, 3, -3)] + [place.target(0, d) for d in (1, -1)]
    greeted += [place.beside(dx, other) for dx in range(4) for other in (False, True) if dx or other]
    for device in greeted:
        pl.semaphore_signal(barrier, inc=1, device_id=device, device_id_type=MESH)
    for copy in fetch[:RB]:
        copy.wait()
    pl.semaphore_wait(barrier, len(greeted))

    asked = [remote(wanted, wanted_by.at[i], sends.at[5 + i], want_recv.at[i], place.target(d, 0)) for i, d in ((1, 1), (0, -1))]
    to_index = pltpu.make_async_copy(index_row, index_ref, local.at[7])
    to_table = pltpu.make_async_copy(wanted_by, table, local.at[8])

    weights = ColGather(place, w1_ref, w1_all, feat, sends.at[2], col_recv.at[0])
    peers = [(dx, other) for dx in range(4) for other in (False, True) if dx or other]

    def bias_copy(index, dx, other, coming):
        core = 1 - place.core if other else place.core
        x = (place.x - dx + 4) % 4 if coming else place.x
        source = x * 2 + (core if coming else place.core)
        rows = b1_all.at[pl.ds(source * feat, feat)]
        return remote(b1_own, rows, sends.at[4], bias_recv.at[index], place.beside(dx, other))

    def between(count):
        if count == 0:
            weights.begin()
            first, last, index = tile_plan(place, colrow_ref[...], count_ref[0])
            lane = lax.broadcasted_iota(jnp.int32, wanted.shape, 1)
            wanted[...] = jnp.where(lane == 0, first, last)
            index_row[:, 0 : index.shape[1]] = jnp.broadcast_to(index, (8, index.shape[1]))
            b1_own[...] = jnp.broadcast_to(as_column(b1_ref[...]), b1_own.shape)
            b1_all[pl.ds(place.col * feat, feat)] = b1_own[...]
            for copy in asked:
                copy.start()
            to_index.start()
            for index, (dx, other) in enumerate(peers):
                bias_copy(index, dx, other, False).start()
        elif count == TABLE:
            for copy in asked:
                copy.wait()
            to_table.start()
        elif count == TABLE + 1:
            to_table.wait()
        elif count == TABLE + 5:
            weights.forward(0)
        elif count == TABLE + 12:
            weights.forward(1)

    node_gather(place, held1, stage, table, sends.at[0], recv1, recv1.at[SLOTS], TABLE + 1, between)
    to_index.wait()
    weights.finish()
    for index, (dx, other) in enumerate(peers):
        bias_copy(index, dx, other, True).wait_recv()
    sent = b1_all.at[pl.ds(0, len(peers) * feat)]
    remote(sent, sent, sends.at[4], bias_recv.at[0], (place.node, place.col)).wait_send()
    for copy in fetch[RB:]:
        copy.wait()

    live = count_ref[0]
    acc = tile_sum(index_ref, rows_ref, live, held1, tiles)
    for b in range(RB):
        y_own[:, b * BLK : (b + 1) * BLK] = acc[b * feat : (b + 1) * feat].astype(y_own.dtype)
    y_all[pl.ds(place.col * feat, feat)] = y_own[...]
    exchange = ColGather(place, y_own, y_all, feat, sends.at[3], col_recv.at[1])
    exchange.begin()
    exchange.forward(0)
    exchange.forward(1)
    exchange.finish()

    wide = HALF * BLK
    step_rows = 128
    for n in range(RB // HALF):
        columns = pl.ds(n * wide, wide)
        total = jnp.zeros((feat, wide), jnp.float32)
        for m in range(w1_all.shape[0] // step_rows):
            span = pl.ds(m * step_rows, step_rows)
            z = jnp.dot(w1_all[span, :], y_all[:, columns], preferred_element_type=jnp.float32)
            bias = b1_all[span, :]
            h = jnp.maximum(z + jnp.concatenate([bias] * HALF, axis=1), 0.0).astype(jnp.bfloat16)
            total += jnp.dot(w2[:, span], h, preferred_element_type=jnp.float32)
        for k in range(HALF):
            held2[place.node * RB + n * HALF + k] = total[:, k * BLK : (k + 1) * BLK].astype(jnp.bfloat16)

    node_gather(place, held2, stage, table, sends.at[1], recv2, recv2.at[SLOTS])
    acc = tile_sum(index_ref, rows_ref, live, held2, tiles)
    bias = as_column(b2_ref[...])
    for b in range(RB):
        out_ref[:, b * BLK : (b + 1) * BLK] = acc[b * feat : (b + 1) * feat] + bias


def body(x_t, adj_tiles, tile_rows, tile_cols, tile_counts, w_first, b_first, w_second, b_second):
    feat, nodes = x_t.shape
    channels = w_first.shape[1]
    pairs = len(ROWS) * SIDE * CAP
    smem = pl.BlockSpec(memory_space=pltpu.SMEM)
    vmem = pl.BlockSpec(memory_space=pltpu.VMEM)
    hbm = pl.BlockSpec(memory_space=pl.ANY)
    dma = pltpu.SemaphoreType.DMA
    bf16 = jnp.bfloat16
    return pl.pallas_call(
        kernel,
        out_shape=jax.ShapeDtypeStruct((feat, nodes), jnp.float32),
        in_specs=[vmem, smem, smem, hbm, hbm, hbm, vmem, hbm, vmem],
        out_specs=vmem,
        scratch_shapes=[
            pltpu.VMEM((FULL + pairs, feat, BLK), bf16),
            pltpu.VMEM((FULL + pairs, feat, BLK), bf16),
            pltpu.VMEM(adj_tiles.shape, bf16),
            pltpu.VMEM((channels, channels), bf16),
            pltpu.VMEM((feat, channels), bf16),
            pltpu.VMEM((feat, BLK), jnp.float32),
            pltpu.VMEM((channels, BLK), jnp.float32),
            pltpu.VMEM((feat, nodes), bf16),
            pltpu.VMEM((channels, nodes), bf16),
            pltpu.VMEM((pairs, feat, BLK), bf16),
            pltpu.VMEM((SIDE * SIDE, BLK), jnp.int32),
            pltpu.VMEM((2, SIDE * SIDE, BLK), jnp.int32),
            pltpu.VMEM((8, BLK), jnp.int32),
            pltpu.SMEM((2, SIDE * SIDE, BLK), jnp.int32),
            pltpu.SMEM((8, BLK), jnp.int32),
            dma((SLOTS + 1,)),
            dma((SLOTS + 1,)),
            dma((2, 7)),
            dma((7,)),
            dma((2,)),
            dma((7,)),
            dma((9,)),
        ],
        compiler_params=pltpu.CompilerParams(collective_id=0, has_side_effects=True),
    )(tile_cols[None, :], tile_rows, tile_counts, x_t, adj_tiles, w_first, b_first[None, :], w_second, b_second[None, :])


def solution(mesh):
    return jax.shard_map(
        body,
        mesh=mesh,
        in_specs=(
            P("col", "node"),
            P("node", None, None),
            P("node"),
            P("node"),
            P("node"),
            P("col", None),
            P("col"),
            P("col", None),
            P("col"),
        ),
        out_specs=P("col", "node"),
        check_vma=False,
    )
```

```python
import heapq
import itertools

import jax
import jax.numpy as jnp
from jax import lax
from jax.experimental import pallas as pl
from jax.experimental.pallas import tpu as pltpu
from jax.sharding import PartitionSpec as P

MESH = pl.DeviceIdType.MESH
BLK = 128
RB = 4
GROUP = 32
SIDE = 8
FAR, NEAR = 4, 3
HALF = 2
CAP = 2
WIRE, BASE, HOP = 0.6, 0.9, 0.5
TABLE = 2
PARTS = 2
SLOTS = 64


SPINES = (0, 3, -3)
BESIDE = {0: (1, -1), 3: (1, -1), -3: (1,)}
ROWS = (1, -1, 2, 4, -2)
SPANS = ((-1, 0), (1, 2), (-2, -2), (-3, -3), (3, 3), (4, 4))
FULL = SIDE * SIDE * RB


def onward(at):
    a, b = at
    out = []
    if b == 2 and a:
        out += [(a, 4), (a, 3)]
    elif 0 <= b < FAR and not (b == 3 and a):
        out.append((a, b + 1))
    if -NEAR < b <= 0:
        out.append((a, b - 1))
    return out + ([(d, 0) for d in SPINES if d] if at == (0, 0) else [])


def arrival_order():
    wire, base, hop = WIRE, BASE, HOP
    free = {}
    tick = itertools.count()
    events = [(0.0, next(tick), (0, 0))]
    order = []
    while events:
        now, _, at = heapq.heappop(events)
        order.append(at)
        for there in onward(at):
            da, db = there[0] - at[0], there[1] - at[1]
            link = (da != 0, da + db > 0)
            start = max(now, free.get(link, 0.0))
            free[link] = start + wire * abs(da + db)
            heapq.heappush(events, (start + wire + base + hop * abs(da + db), next(tick), there))
    return order


def slot_of(at):
    return (at[0] + NEAR) * SIDE + at[1] + NEAR


class Place:
    def __init__(self):
        self.node, self.col = lax.axis_index("node"), lax.axis_index("col")
        y, z = self.node // SIDE, self.node % SIDE
        self.x, self.core = self.col // 2, self.col % 2
        self.u, self.v = y + (z - y) * self.core, z + (y - z) * self.core
        across, along = SIDE - (SIDE - 1) * self.core, 1 + (SIDE - 1) * self.core
        steps = range(-FAR, FAR + 1)
        self.us = {a: (self.u + a + SIDE) % SIDE * across for a in steps}
        self.vs = {b: (self.v - b + SIDE) % SIDE * along for b in steps}

    def source(self, at):
        return self.us[at[0]] + self.vs[at[1]]

    def target(self, da, db):
        return (self.us[-da] + self.vs[-db], self.col)

    def beside(self, dx, other):
        core = 1 - self.core if other else self.core
        return (self.node, (self.x + dx) % 4 * 2 + core)


def remote(src, dst, send, recv, device):
    return pltpu.make_async_remote_copy(
        src_ref=src, dst_ref=dst, send_sem=send, recv_sem=recv, device_id=device, device_id_type=MESH
    )


def pair_at(a, b):
    return (ROWS.index(a) * SIDE + b + NEAR) * CAP


def node_gather(place, held, stage, table, send, recv, ends, start=1, between=None):
    here = (place.node, place.col)
    picked = set()
    waiting = []

    def pick(at):
        a, b = at
        base = place.source(at) * RB
        blocks = [held[base + k] for k in range(RB)]
        picked.add(at)
        copies = []
        low, high = next(span for span in SPANS if span[0] <= b <= span[1])
        for da in BESIDE[a]:
            for lane in range(CAP):
                want = table[(1 - da) // 2, place.source(at), lane]
                block = blocks[RB - 1]
                for k in range(RB - 1):
                    block = jnp.where(want == k, blocks[k], block)
                stage[pair_at(a + da, b) + lane] = block
            if all((a, other) in picked for other in range(low, high + 1)):
                first, size = pair_at(a + da, low), CAP * (high + 1 - low)
                pairs = held.at[pl.ds(FULL + first, size)]
                copies.append(remote(stage.at[pl.ds(first, size)], pairs, send, ends, place.target(da, 0)))
        return copies

    order = arrival_order()
    for count, at in enumerate(order):
        rows = held.at[pl.ds(place.source(at) * RB, RB)]
        if at != (0, 0):
            remote(rows, rows, send, recv.at[slot_of(at)], here).wait_recv()
        for there in onward(at):
            remote(rows, rows, send, recv.at[slot_of(there)], place.target(there[0] - at[0], there[1] - at[1])).start()
        if between is not None:
            between(count)
        if count >= start:
            for old in waiting + [at]:
                for copy in pick(old):
                    copy.start()
            waiting = []
        else:
            waiting.append(at)
    for at in waiting:
        for copy in pick(at):
            copy.start()
    came = held.at[pl.ds(0, len(ROWS) * SIDE * CAP)]
    remote(came, came, send, ends, here).wait_recv()
    sent = held.at[pl.ds(0, (len(order) - 1) * RB + len(ROWS) * SIDE * CAP)]
    remote(sent, sent, send, ends, here).wait_send()


class ColGather:
    def __init__(self, place, own, rows, feat, send, recv, shift=0):
        self.place, self.own, self.rows, self.feat, self.send, self.recv = place, own, rows, feat, send, recv
        self.shift, self.size = shift, own.shape[0]

    def cut(self, x, core, part):
        start = (x % 4 * 2 + core) * self.feat
        if part is None:
            return self.rows.at[pl.ds(start + self.shift, self.size)]
        return self.rows.at[pl.ds(start + part * self.half, self.half)]

    def mine(self, part):
        if part is None:
            return self.own
        return self.own.at[pl.ds(part * self.half, self.half)]

    def begin(self):
        p = self.place
        for dx, sem in ((1, 0), (-1, 1), (2, 2)):
            remote(self.own, self.cut(p.x, p.core, None), self.send, self.recv.at[sem], p.beside(dx + 4, False)).start()
        remote(self.own, self.cut(p.x, p.core, None), self.send, self.recv.at[3], p.beside(0, True)).start()

    def wait(self, dx, other, sem):
        p = self.place
        core = 1 - p.core if other else p.core
        rows = self.cut(p.x + dx + 4, core, None)
        remote(rows, rows, self.send, self.recv.at[sem], (p.node, p.col)).wait_recv()
        return rows

    def forward(self, stage):
        p = self.place
        for dx, sem in ((-1, 0), (1, 1)) if stage == 0 else ((2, 2),):
            rows = self.wait(dx, False, sem)
            remote(rows, rows, self.send, self.recv.at[4 + sem], p.beside(0, True)).start()

    def finish(self):
        for dx, sem in ((0, 3), (-1, 4), (1, 5), (2, 6)):
            self.wait(dx, True, sem)
        sent = self.rows.at[pl.ds(0, 7 * self.size)]
        remote(sent, sent, self.send, self.recv.at[0], (self.place.node, self.place.col)).wait_send()


def tile_sum(index_ref, rows_ref, live, gathered, tiles, low, feat):
    total = tiles.shape[0]

    def step(g, acc):
        left, right = [], []
        for k in range(GROUP):
            t = g * GROUP + k
            block = gathered[index_ref[0, t], low : low + feat]
            row = jnp.where(t < live, rows_ref[t], RB)
            zero = jnp.zeros_like(block)
            left.append(jnp.concatenate([jnp.where(row == b, block, zero) for b in range(RB)], axis=0))
            right.append(tiles[t])
        return acc + lax.dot_general(
            jnp.concatenate(left, axis=1),
            jnp.concatenate(right, axis=1),
            (((1,), (1,)), ((), ())),
            preferred_element_type=jnp.float32,
        )

    return lax.fori_loop(0, total // GROUP, step, jnp.zeros((RB * feat, BLK), jnp.float32))


def as_column(row):
    size = row.shape[1]
    square = jnp.broadcast_to(row, (size, size))
    same = lax.broadcasted_iota(jnp.int32, (size, size), 0) == lax.broadcasted_iota(jnp.int32, (size, size), 1)
    return jnp.sum(jnp.where(same, square, 0.0), axis=1, keepdims=True)


def tile_plan(place, cols, live):
    total, nodes = cols.shape[1], SIDE * SIDE
    node, block = cols >> 2, cols & (RB - 1)
    alive = lax.broadcasted_iota(jnp.int32, (1, total), 1) < live
    node = jnp.where(alive, node, nodes)
    hit = lax.broadcasted_iota(jnp.int32, (nodes, total), 0) == node
    first = jnp.min(jnp.where(hit, block, RB - 1).astype(jnp.float32), axis=1, keepdims=True).astype(jnp.int32)
    last = jnp.max(jnp.where(hit, block, 0).astype(jnp.float32), axis=1, keepdims=True).astype(jnp.int32)
    lowest = jnp.min(jnp.where(hit, first, RB - 1).astype(jnp.float32), axis=0, keepdims=True).astype(jnp.int32)
    owner = cols >> 2
    u = (owner >> 3) * (1 - place.core) + (owner & (SIDE - 1)) * place.core
    a = (u - place.u + SIDE) & (SIDE - 1)
    line = (a == 0) | (a == 3) | (a == SIDE - 3)
    v = (owner & (SIDE - 1)) * (1 - place.core) + (owner >> 3) * place.core
    row = jnp.zeros_like(a)
    for i, at in enumerate(ROWS):
        row = jnp.where(a == at % SIDE, i, row)
    pair = (row * SIDE + ((place.v - v + NEAR) & (SIDE - 1))) * CAP
    beside = FULL + pair + jnp.where(block == lowest, 0, 1)
    return first, last, jnp.where(line, owner * RB + block, beside)


def kernel(
    colrow_ref, rows_ref, count_ref, x_ref, adj_ref, w1_ref, b1_ref, w2_ref, b2_ref, out_ref,
    held1, held2, tiles, w1_all, w2, b1_own, b1_all, y_own, y_all,
    stage, wanted, wanted_by, index_row, table, index_ref,
    recv1, recv2, col_recv, bias_recv, want_recv, sends, local,
):
    feat = y_own.shape[0]
    place = Place()
    fetch = [
        pltpu.make_async_copy(x_ref.at[:, pl.ds(k * BLK, BLK)], held1.at[place.node * RB + k], local.at[k]) for k in range(RB)
    ]
    fetch += [
        pltpu.make_async_copy(adj_ref, tiles, local.at[4]),
        pltpu.make_async_copy(w2_ref, w2, local.at[5]),
        pltpu.make_async_copy(w1_ref, w1_all.at[pl.ds(place.col * feat, feat)], local.at[6]),
    ]
    for copy in fetch:
        copy.start()

    barrier = pltpu.get_barrier_semaphore()
    greeted = [place.target(d, 0) for d in (1, -1, 3, -3)] + [place.target(0, d) for d in (1, -1, 2, -2)]
    greeted += [place.beside(dx, other) for dx in range(4) for other in (False, True) if dx or other]
    for device in greeted:
        pl.semaphore_signal(barrier, inc=1, device_id=device, device_id_type=MESH)
    for copy in fetch[:RB]:
        copy.wait()
    pl.semaphore_wait(barrier, len(greeted))

    asked = [remote(wanted, wanted_by.at[i], sends.at[5 + i], want_recv.at[i], place.target(d, 0)) for i, d in ((1, 1), (0, -1))]
    to_index = pltpu.make_async_copy(index_row, index_ref, local.at[7])
    to_table = pltpu.make_async_copy(wanted_by, table, local.at[8])

    weights = ColGather(place, w1_ref, w1_all, feat, sends.at[2], col_recv.at[0])
    peers = [(dx, other) for dx in range(4) for other in (False, True) if dx or other]

    def bias_copy(index, dx, other, coming):
        core = 1 - place.core if other else place.core
        x = (place.x - dx + 4) % 4 if coming else place.x
        source = x * 2 + (core if coming else place.core)
        rows = b1_all.at[pl.ds(source * feat, feat)]
        return remote(b1_own, rows, sends.at[4], bias_recv.at[index], place.beside(dx, other))

    def between(count):
        if count == 0:
            weights.begin()
            first, last, index = tile_plan(place, colrow_ref[...], count_ref[0])
            lane = lax.broadcasted_iota(jnp.int32, wanted.shape, 1)
            wanted[...] = jnp.where(lane == 0, first, last)
            index_row[:, 0 : index.shape[1]] = jnp.broadcast_to(index, (8, index.shape[1]))
            b1_own[...] = jnp.broadcast_to(as_column(b1_ref[...]), b1_own.shape)
            b1_all[pl.ds(place.col * feat, feat)] = b1_own[...]
            for copy in asked:
                copy.start()
            to_index.start()
            for index, (dx, other) in enumerate(peers):
                bias_copy(index, dx, other, False).start()
        elif count == TABLE:
            for copy in asked:
                copy.wait()
            to_table.start()
        elif count == TABLE + 1:
            to_table.wait()
        elif count == TABLE + 5:
            weights.forward(0)
        elif count == TABLE + 12:
            weights.forward(1)

    node_gather(place, held1, stage, table, sends.at[0], recv1, recv1.at[SLOTS], TABLE + 1, between)
    to_index.wait()
    weights.finish()
    for index, (dx, other) in enumerate(peers):
        bias_copy(index, dx, other, True).wait_recv()
    sent = b1_all.at[pl.ds(0, len(peers) * feat)]
    remote(sent, sent, sends.at[4], bias_recv.at[0], (place.node, place.col)).wait_send()
    for copy in fetch[RB:]:
        copy.wait()

    live = count_ref[0]
    exchanges = []
    part = feat // PARTS
    for p in range(PARTS):
        acc = tile_sum(index_ref, rows_ref, live, held1, tiles, p * part, part)
        for b in range(RB):
            y_own[p * part : (p + 1) * part, b * BLK : (b + 1) * BLK] = acc[b * part : (b + 1) * part].astype(y_own.dtype)
        y_all[pl.ds(place.col * feat + p * part, part)] = y_own[p * part : (p + 1) * part]
        own = y_own.at[pl.ds(p * part, part)]
        exchanges.append(ColGather(place, own, y_all, feat, sends.at[7 + p], col_recv.at[1 + p], p * part))
        exchanges[-1].begin()
    for leg in (0, 1):
        for exchange in exchanges:
            exchange.forward(leg)
    for exchange in exchanges:
        exchange.finish()

    wide = HALF * BLK
    step_rows = 128
    for n in range(RB // HALF):
        columns = pl.ds(n * wide, wide)
        total = jnp.zeros((feat, wide), jnp.float32)
        for m in range(w1_all.shape[0] // step_rows):
            span = pl.ds(m * step_rows, step_rows)
            z = jnp.dot(w1_all[span, :], y_all[:, columns], preferred_element_type=jnp.float32)
            bias = b1_all[span, :]
            h = jnp.maximum(z + jnp.concatenate([bias] * HALF, axis=1), 0.0).astype(jnp.bfloat16)
            total += jnp.dot(w2[:, span], h, preferred_element_type=jnp.float32)
        for k in range(HALF):
            held2[place.node * RB + n * HALF + k] = total[:, k * BLK : (k + 1) * BLK].astype(jnp.bfloat16)

    node_gather(place, held2, stage, table, sends.at[1], recv2, recv2.at[SLOTS])
    acc = tile_sum(index_ref, rows_ref, live, held2, tiles, 0, feat)
    bias = as_column(b2_ref[...])
    for b in range(RB):
        out_ref[:, b * BLK : (b + 1) * BLK] = acc[b * feat : (b + 1) * feat] + bias


def body(x_t, adj_tiles, tile_rows, tile_cols, tile_counts, w_first, b_first, w_second, b_second):
    feat, nodes = x_t.shape
    channels = w_first.shape[1]
    pairs = len(ROWS) * SIDE * CAP
    smem = pl.BlockSpec(memory_space=pltpu.SMEM)
    vmem = pl.BlockSpec(memory_space=pltpu.VMEM)
    hbm = pl.BlockSpec(memory_space=pl.ANY)
    dma = pltpu.SemaphoreType.DMA
    bf16 = jnp.bfloat16
    return pl.pallas_call(
        kernel,
        out_shape=jax.ShapeDtypeStruct((feat, nodes), jnp.float32),
        in_specs=[vmem, smem, smem, hbm, hbm, hbm, vmem, hbm, vmem],
        out_specs=vmem,
        scratch_shapes=[
            pltpu.VMEM((FULL + pairs, feat, BLK), bf16),
            pltpu.VMEM((FULL + pairs, feat, BLK), bf16),
            pltpu.VMEM(adj_tiles.shape, bf16),
            pltpu.VMEM((channels, channels), bf16),
            pltpu.VMEM((feat, channels), bf16),
            pltpu.VMEM((feat, BLK), jnp.float32),
            pltpu.VMEM((channels, BLK), jnp.float32),
            pltpu.VMEM((feat, nodes), bf16),
            pltpu.VMEM((channels, nodes), bf16),
            pltpu.VMEM((pairs, feat, BLK), bf16),
            pltpu.VMEM((SIDE * SIDE, BLK), jnp.int32),
            pltpu.VMEM((2, SIDE * SIDE, BLK), jnp.int32),
            pltpu.VMEM((8, BLK), jnp.int32),
            pltpu.SMEM((2, SIDE * SIDE, BLK), jnp.int32),
            pltpu.SMEM((8, BLK), jnp.int32),
            dma((SLOTS + 1,)),
            dma((SLOTS + 1,)),
            dma((1 + PARTS, 7)),
            dma((7,)),
            dma((2,)),
            dma((7 + PARTS,)),
            dma((9,)),
        ],
        compiler_params=pltpu.CompilerParams(collective_id=0, has_side_effects=True),
    )(tile_cols[None, :], tile_rows, tile_counts, x_t, adj_tiles, w_first, b_first[None, :], w_second, b_second[None, :])


def solution(mesh):
    return jax.shard_map(
        body,
        mesh=mesh,
        in_specs=(
            P("col", "node"),
            P("node", None, None),
            P("node"),
            P("node"),
            P("node"),
            P("col", None),
            P("col"),
            P("col", None),
            P("col"),
        ),
        out_specs=P("col", "node"),
        check_vma=False,
    )
```

```python
import heapq
import itertools

import jax
import jax.numpy as jnp
from jax import lax
from jax.experimental import pallas as pl
from jax.experimental.pallas import tpu as pltpu
from jax.sharding import PartitionSpec as P

MESH = pl.DeviceIdType.MESH
BLK = 128
RB = 4
GROUP = 32
SIDE = 8
FAR, NEAR = 4, 3
HALF = 2
CAP = 2
WIRE, BASE, HOP = 0.6, 0.9, 0.5
TABLE = 2
PARTS = 2
SLOTS = 64


SPINES = (0, 3, -3)
BESIDE = {0: (1, -1), 3: (1, -1), -3: (1,)}
ROWS = (1, -1, 2, 4, -2)
SPANS = ((-1, 0), (1, 2), (-2, -2), (-3, -3), (3, 3), (4, 4))
FULL = SIDE * SIDE * RB


def onward(at):
    a, b = at
    out = []
    if b == 2 and a:
        out += [(a, 4), (a, 3)]
    elif 0 <= b < FAR and not (b == 3 and a):
        out.append((a, b + 1))
    if -NEAR < b <= 0:
        out.append((a, b - 1))
    return out + ([(d, 0) for d in SPINES if d] if at == (0, 0) else [])


def arrival_order():
    wire, base, hop = WIRE, BASE, HOP
    free = {}
    tick = itertools.count()
    events = [(0.0, next(tick), (0, 0))]
    order = []
    while events:
        now, _, at = heapq.heappop(events)
        order.append(at)
        for there in onward(at):
            da, db = there[0] - at[0], there[1] - at[1]
            link = (da != 0, da + db > 0)
            start = max(now, free.get(link, 0.0))
            free[link] = start + wire * abs(da + db)
            heapq.heappush(events, (start + wire + base + hop * abs(da + db), next(tick), there))
    return order


def slot_of(at):
    return (at[0] + NEAR) * SIDE + at[1] + NEAR


class Place:
    def __init__(self):
        self.node, self.col = lax.axis_index("node"), lax.axis_index("col")
        y, z = self.node // SIDE, self.node % SIDE
        self.x, self.core = self.col // 2, self.col % 2
        self.u, self.v = y + (z - y) * self.core, z + (y - z) * self.core
        across, along = SIDE - (SIDE - 1) * self.core, 1 + (SIDE - 1) * self.core
        steps = range(-FAR, FAR + 1)
        self.us = {a: (self.u + a + SIDE) % SIDE * across for a in steps}
        self.vs = {b: (self.v - b + SIDE) % SIDE * along for b in steps}

    def source(self, at):
        return self.us[at[0]] + self.vs[at[1]]

    def target(self, da, db):
        return (self.us[-da] + self.vs[-db], self.col)

    def beside(self, dx, other):
        core = 1 - self.core if other else self.core
        return (self.node, (self.x + dx) % 4 * 2 + core)


def remote(src, dst, send, recv, device):
    return pltpu.make_async_remote_copy(
        src_ref=src, dst_ref=dst, send_sem=send, recv_sem=recv, device_id=device, device_id_type=MESH
    )


def pair_at(a, b):
    return (ROWS.index(a) * SIDE + b + NEAR) * CAP


def node_gather(place, held, stage, table, send, recv, ends, start=1, between=None):
    here = (place.node, place.col)
    picked = set()
    waiting = []

    def pick(at):
        a, b = at
        base = place.source(at) * RB
        blocks = [held[base + k] for k in range(RB)]
        picked.add(at)
        copies = []
        low, high = next(span for span in SPANS if span[0] <= b <= span[1])
        for da in BESIDE[a]:
            for lane in range(CAP):
                want = table[(1 - da) // 2, place.source(at), lane]
                block = blocks[RB - 1]
                for k in range(RB - 1):
                    block = jnp.where(want == k, blocks[k], block)
                stage[pair_at(a + da, b) + lane] = block
            if all((a, other) in picked for other in range(low, high + 1)):
                first, size = pair_at(a + da, low), CAP * (high + 1 - low)
                pairs = held.at[pl.ds(FULL + first, size)]
                copies.append(remote(stage.at[pl.ds(first, size)], pairs, send, ends, place.target(da, 0)))
        return copies

    order = arrival_order()
    for count, at in enumerate(order):
        rows = held.at[pl.ds(place.source(at) * RB, RB)]
        if at != (0, 0):
            remote(rows, rows, send, recv.at[slot_of(at)], here).wait_recv()
        for there in onward(at):
            remote(rows, rows, send, recv.at[slot_of(there)], place.target(there[0] - at[0], there[1] - at[1])).start()
        if between is not None:
            between(count)
        if count >= start:
            for old in waiting + [at]:
                for copy in pick(old):
                    copy.start()
            waiting = []
        else:
            waiting.append(at)
    for at in waiting:
        for copy in pick(at):
            copy.start()
    came = held.at[pl.ds(0, len(ROWS) * SIDE * CAP)]
    remote(came, came, send, ends, here).wait_recv()
    sent = held.at[pl.ds(0, (len(order) - 1) * RB + len(ROWS) * SIDE * CAP)]
    remote(sent, sent, send, ends, here).wait_send()


class ColGather:
    def __init__(self, place, own, rows, feat, send, recv, shift=0):
        self.place, self.own, self.rows, self.feat, self.send, self.recv = place, own, rows, feat, send, recv
        self.shift, self.size = shift, own.shape[0]

    def cut(self, x, core, part):
        start = (x % 4 * 2 + core) * self.feat
        if part is None:
            return self.rows.at[pl.ds(start + self.shift, self.size)]
        return self.rows.at[pl.ds(start + part * self.half, self.half)]

    def mine(self, part):
        if part is None:
            return self.own
        return self.own.at[pl.ds(part * self.half, self.half)]

    def begin(self):
        p = self.place
        for dx, sem in ((1, 0), (-1, 1), (2, 2)):
            remote(self.own, self.cut(p.x, p.core, None), self.send, self.recv.at[sem], p.beside(dx + 4, False)).start()
        remote(self.own, self.cut(p.x, p.core, None), self.send, self.recv.at[3], p.beside(0, True)).start()

    def wait(self, dx, other, sem):
        p = self.place
        core = 1 - p.core if other else p.core
        rows = self.cut(p.x + dx + 4, core, None)
        remote(rows, rows, self.send, self.recv.at[sem], (p.node, p.col)).wait_recv()
        return rows

    def forward(self, stage):
        p = self.place
        for dx, sem in ((-1, 0), (1, 1)) if stage == 0 else ((2, 2),):
            rows = self.wait(dx, False, sem)
            remote(rows, rows, self.send, self.recv.at[4 + sem], p.beside(0, True)).start()

    def finish(self):
        for dx, sem in ((0, 3), (-1, 4), (1, 5), (2, 6)):
            self.wait(dx, True, sem)
        sent = self.rows.at[pl.ds(0, 7 * self.size)]
        remote(sent, sent, self.send, self.recv.at[0], (self.place.node, self.place.col)).wait_send()


def tile_sum(index_ref, rows_ref, live, gathered, tiles, low, feat):
    total = tiles.shape[0]

    def step(g, acc):
        left, right = [], []
        for k in range(GROUP):
            t = g * GROUP + k
            block = gathered[index_ref[0, t], low : low + feat]
            row = jnp.where(t < live, rows_ref[t], RB)
            zero = jnp.zeros_like(block)
            left.append(jnp.concatenate([jnp.where(row == b, block, zero) for b in range(RB)], axis=0))
            right.append(tiles[t])
        return acc + lax.dot_general(
            jnp.concatenate(left, axis=1),
            jnp.concatenate(right, axis=1),
            (((1,), (1,)), ((), ())),
            preferred_element_type=jnp.float32,
        )

    return lax.fori_loop(0, total // GROUP, step, jnp.zeros((RB * feat, BLK), jnp.float32))


def as_column(row):
    size = row.shape[1]
    square = jnp.broadcast_to(row, (size, size))
    same = lax.broadcasted_iota(jnp.int32, (size, size), 0) == lax.broadcasted_iota(jnp.int32, (size, size), 1)
    return jnp.sum(jnp.where(same, square, 0.0), axis=1, keepdims=True)


def tile_plan(place, cols, live):
    total, nodes = cols.shape[1], SIDE * SIDE
    node, block = cols >> 2, cols & (RB - 1)
    alive = lax.broadcasted_iota(jnp.int32, (1, total), 1) < live
    node = jnp.where(alive, node, nodes)
    hit = lax.broadcasted_iota(jnp.int32, (nodes, total), 0) == node
    first = jnp.min(jnp.where(hit, block, RB - 1).astype(jnp.float32), axis=1, keepdims=True).astype(jnp.int32)
    last = jnp.max(jnp.where(hit, block, 0).astype(jnp.float32), axis=1, keepdims=True).astype(jnp.int32)
    lowest = jnp.min(jnp.where(hit, first, RB - 1).astype(jnp.float32), axis=0, keepdims=True).astype(jnp.int32)
    owner = cols >> 2
    u = (owner >> 3) * (1 - place.core) + (owner & (SIDE - 1)) * place.core
    a = (u - place.u + SIDE) & (SIDE - 1)
    line = (a == 0) | (a == 3) | (a == SIDE - 3)
    v = (owner & (SIDE - 1)) * (1 - place.core) + (owner >> 3) * place.core
    row = jnp.zeros_like(a)
    for i, at in enumerate(ROWS):
        row = jnp.where(a == at % SIDE, i, row)
    pair = (row * SIDE + ((place.v - v + NEAR) & (SIDE - 1))) * CAP
    beside = FULL + pair + jnp.where(block == lowest, 0, 1)
    return first, last, jnp.where(line, owner * RB + block, beside)


def kernel(
    colrow_ref, rows_ref, count_ref, x_ref, adj_ref, w1_ref, b1_ref, w2_ref, b2_ref, out_ref,
    held1, held2, tiles, w1_all, w2, b1_own, b1_all, y_own, y_all,
    stage, wanted, wanted_by, index_row, table, index_ref,
    recv1, recv2, col_recv, bias_recv, want_recv, sends, local,
):
    feat = y_own.shape[0]
    place = Place()
    fetch = [
        pltpu.make_async_copy(x_ref.at[:, pl.ds(k * BLK, BLK)], held1.at[place.node * RB + k], local.at[k]) for k in range(RB)
    ]
    fetch += [
        pltpu.make_async_copy(adj_ref, tiles, local.at[4]),
        pltpu.make_async_copy(w2_ref, w2, local.at[5]),
        pltpu.make_async_copy(w1_ref, w1_all.at[pl.ds(place.col * feat, feat)], local.at[6]),
    ]
    for copy in fetch:
        copy.start()

    barrier = pltpu.get_barrier_semaphore()
    greeted = [place.target(d, 0) for d in (1, -1, 3, -3)] + [place.target(0, d) for d in (1, -1, 2, -2)]
    greeted += [place.beside(dx, other) for dx in range(4) for other in (False, True) if dx or other]
    for device in greeted:
        pl.semaphore_signal(barrier, inc=1, device_id=device, device_id_type=MESH)
    for copy in fetch[:RB]:
        copy.wait()
    pl.semaphore_wait(barrier, len(greeted))

    asked = [remote(wanted, wanted_by.at[i], sends.at[5 + i], want_recv.at[i], place.target(d, 0)) for i, d in ((1, 1), (0, -1))]
    to_index = pltpu.make_async_copy(index_row, index_ref, local.at[7])
    to_table = pltpu.make_async_copy(wanted_by, table, local.at[8])

    weights = ColGather(place, w1_ref, w1_all, feat, sends.at[2], col_recv.at[0])
    peers = [(dx, other) for dx in range(4) for other in (False, True) if dx or other]

    def bias_copy(index, dx, other, coming):
        core = 1 - place.core if other else place.core
        x = (place.x - dx + 4) % 4 if coming else place.x
        source = x * 2 + (core if coming else place.core)
        rows = b1_all.at[pl.ds(source * feat, feat)]
        return remote(b1_own, rows, sends.at[4], bias_recv.at[index], place.beside(dx, other))

    def between(count):
        if count == 0:
            first, last, index = tile_plan(place, colrow_ref[...], count_ref[0])
            lane = lax.broadcasted_iota(jnp.int32, wanted.shape, 1)
            wanted[...] = jnp.where(lane == 0, first, last)
            index_row[:, 0 : index.shape[1]] = jnp.broadcast_to(index, (8, index.shape[1]))
            b1_own[...] = jnp.broadcast_to(as_column(b1_ref[...]), b1_own.shape)
            b1_all[pl.ds(place.col * feat, feat)] = b1_own[...]
            for copy in asked:
                copy.start()
            to_index.start()
            for index, (dx, other) in enumerate(peers):
                bias_copy(index, dx, other, False).start()
            weights.begin()
        elif count == TABLE:
            for copy in asked:
                copy.wait()
            to_table.start()
        elif count == TABLE + 1:
            to_table.wait()
        elif count == TABLE + 5:
            weights.forward(0)
        elif count == TABLE + 12:
            weights.forward(1)

    node_gather(place, held1, stage, table, sends.at[0], recv1, recv1.at[SLOTS], TABLE + 1, between)
    to_index.wait()
    weights.finish()
    for index, (dx, other) in enumerate(peers):
        bias_copy(index, dx, other, True).wait_recv()
    sent = b1_all.at[pl.ds(0, len(peers) * feat)]
    remote(sent, sent, sends.at[4], bias_recv.at[0], (place.node, place.col)).wait_send()
    for copy in fetch[RB:]:
        copy.wait()

    live = count_ref[0]
    exchanges = []
    part = feat // PARTS
    for p in range(PARTS):
        acc = tile_sum(index_ref, rows_ref, live, held1, tiles, p * part, part)
        for b in range(RB):
            y_own[p * part : (p + 1) * part, b * BLK : (b + 1) * BLK] = acc[b * part : (b + 1) * part].astype(y_own.dtype)
        y_all[pl.ds(place.col * feat + p * part, part)] = y_own[p * part : (p + 1) * part]
        own = y_own.at[pl.ds(p * part, part)]
        exchanges.append(ColGather(place, own, y_all, feat, sends.at[7 + p], col_recv.at[1 + p], p * part))
        exchanges[-1].begin()
    for leg in (0, 1):
        for exchange in exchanges:
            exchange.forward(leg)
    for exchange in exchanges:
        exchange.finish()

    wide = HALF * BLK
    step_rows = 128
    for n in range(RB // HALF):
        columns = pl.ds(n * wide, wide)
        total = jnp.zeros((feat, wide), jnp.float32)
        for m in range(w1_all.shape[0] // step_rows):
            span = pl.ds(m * step_rows, step_rows)
            z = jnp.dot(w1_all[span, :], y_all[:, columns], preferred_element_type=jnp.float32)
            bias = b1_all[span, :]
            h = jnp.maximum(z + jnp.concatenate([bias] * HALF, axis=1), 0.0).astype(jnp.bfloat16)
            total += jnp.dot(w2[:, span], h, preferred_element_type=jnp.float32)
        for k in range(HALF):
            held2[place.node * RB + n * HALF + k] = total[:, k * BLK : (k + 1) * BLK].astype(jnp.bfloat16)

    node_gather(place, held2, stage, table, sends.at[1], recv2, recv2.at[SLOTS])
    acc = tile_sum(index_ref, rows_ref, live, held2, tiles, 0, feat)
    bias = as_column(b2_ref[...])
    for b in range(RB):
        out_ref[:, b * BLK : (b + 1) * BLK] = acc[b * feat : (b + 1) * feat] + bias


def body(x_t, adj_tiles, tile_rows, tile_cols, tile_counts, w_first, b_first, w_second, b_second):
    feat, nodes = x_t.shape
    channels = w_first.shape[1]
    pairs = len(ROWS) * SIDE * CAP
    smem = pl.BlockSpec(memory_space=pltpu.SMEM)
    vmem = pl.BlockSpec(memory_space=pltpu.VMEM)
    hbm = pl.BlockSpec(memory_space=pl.ANY)
    dma = pltpu.SemaphoreType.DMA
    bf16 = jnp.bfloat16
    return pl.pallas_call(
        kernel,
        out_shape=jax.ShapeDtypeStruct((feat, nodes), jnp.float32),
        in_specs=[vmem, smem, smem, hbm, hbm, hbm, vmem, hbm, vmem],
        out_specs=vmem,
        scratch_shapes=[
            pltpu.VMEM((FULL + pairs, feat, BLK), bf16),
            pltpu.VMEM((FULL + pairs, feat, BLK), bf16),
            pltpu.VMEM(adj_tiles.shape, bf16),
            pltpu.VMEM((channels, channels), bf16),
            pltpu.VMEM((feat, channels), bf16),
            pltpu.VMEM((feat, BLK), jnp.float32),
            pltpu.VMEM((channels, BLK), jnp.float32),
            pltpu.VMEM((feat, nodes), bf16),
            pltpu.VMEM((channels, nodes), bf16),
            pltpu.VMEM((pairs, feat, BLK), bf16),
            pltpu.VMEM((SIDE * SIDE, BLK), jnp.int32),
            pltpu.VMEM((2, SIDE * SIDE, BLK), jnp.int32),
            pltpu.VMEM((8, BLK), jnp.int32),
            pltpu.SMEM((2, SIDE * SIDE, BLK), jnp.int32),
            pltpu.SMEM((8, BLK), jnp.int32),
            dma((SLOTS + 1,)),
            dma((SLOTS + 1,)),
            dma((1 + PARTS, 7)),
            dma((7,)),
            dma((2,)),
            dma((7 + PARTS,)),
            dma((9,)),
        ],
        compiler_params=pltpu.CompilerParams(collective_id=0, has_side_effects=True),
    )(tile_cols[None, :], tile_rows, tile_counts, x_t, adj_tiles, w_first, b_first[None, :], w_second, b_second[None, :])


def solution(mesh):
    return jax.shard_map(
        body,
        mesh=mesh,
        in_specs=(
            P("col", "node"),
            P("node", None, None),
            P("node"),
            P("node"),
            P("node"),
            P("col", None),
            P("col"),
            P("col", None),
            P("col"),
        ),
        out_specs=P("col", "node"),
        check_vma=False,
    )
```

```python
import heapq
import itertools

import jax
import jax.numpy as jnp
from jax import lax
from jax.experimental import pallas as pl
from jax.experimental.pallas import tpu as pltpu
from jax.sharding import PartitionSpec as P

MESH = pl.DeviceIdType.MESH
BLK = 128
RB = 4
GROUP = 32
SIDE = 8
FAR, NEAR = 4, 3
HALF = 2
CAP = 2
WIRE, BASE, HOP = 0.6, 0.9, 0.5
TABLE = 2
PARTS = 2
SLOTS = 64


SPINES = (0, 3, -3)
BESIDE = {0: (1, -1), 3: (1, -1), -3: (1,)}
ROWS = (1, -1, 2, 4, -2)
SPANS = ((-1, 0), (1, 2), (-2, -2), (-3, -3), (3, 3), (4, 4))
FULL = SIDE * SIDE * RB


def onward(at):
    a, b = at
    out = []
    if b == 2 and a:
        out += [(a, 4), (a, 3)]
    elif 0 <= b < FAR and not (b == 3 and a):
        out.append((a, b + 1))
    if -NEAR < b <= 0:
        out.append((a, b - 1))
    return out + ([(d, 0) for d in SPINES if d] if at == (0, 0) else [])


def arrival_order():
    wire, base, hop = WIRE, BASE, HOP
    free = {}
    tick = itertools.count()
    events = [(0.0, next(tick), (0, 0))]
    order = []
    while events:
        now, _, at = heapq.heappop(events)
        order.append(at)
        for there in onward(at):
            da, db = there[0] - at[0], there[1] - at[1]
            link = (da != 0, da + db > 0)
            start = max(now, free.get(link, 0.0))
            free[link] = start + wire * abs(da + db)
            heapq.heappush(events, (start + wire + base + hop * abs(da + db), next(tick), there))
    return order


def slot_of(at):
    return (at[0] + NEAR) * SIDE + at[1] + NEAR


class Place:
    def __init__(self):
        self.node, self.col = lax.axis_index("node"), lax.axis_index("col")
        y, z = self.node // SIDE, self.node % SIDE
        self.x, self.core = self.col // 2, self.col % 2
        self.u, self.v = y + (z - y) * self.core, z + (y - z) * self.core
        across, along = SIDE - (SIDE - 1) * self.core, 1 + (SIDE - 1) * self.core
        steps = range(-FAR, FAR + 1)
        self.us = {a: (self.u + a + SIDE) % SIDE * across for a in steps}
        self.vs = {b: (self.v - b + SIDE) % SIDE * along for b in steps}

    def source(self, at):
        return self.us[at[0]] + self.vs[at[1]]

    def target(self, da, db):
        return (self.us[-da] + self.vs[-db], self.col)

    def beside(self, dx, other):
        core = 1 - self.core if other else self.core
        return (self.node, (self.x + dx) % 4 * 2 + core)


def remote(src, dst, send, recv, device):
    return pltpu.make_async_remote_copy(
        src_ref=src, dst_ref=dst, send_sem=send, recv_sem=recv, device_id=device, device_id_type=MESH
    )


def pair_at(a, b):
    return (ROWS.index(a) * SIDE + b + NEAR) * CAP


def node_gather(place, held, stage, table, send, recv, ends, start=1, between=None):
    here = (place.node, place.col)
    picked = set()
    waiting = []

    def pick(at):
        a, b = at
        base = place.source(at) * RB
        blocks = [held[base + k] for k in range(RB)]
        picked.add(at)
        copies = []
        low, high = next(span for span in SPANS if span[0] <= b <= span[1])
        for da in BESIDE[a]:
            for lane in range(CAP):
                want = table[(1 - da) // 2, place.source(at), lane]
                block = blocks[RB - 1]
                for k in range(RB - 1):
                    block = jnp.where(want == k, blocks[k], block)
                stage[pair_at(a + da, b) + lane] = block
            if all((a, other) in picked for other in range(low, high + 1)):
                first, size = pair_at(a + da, low), CAP * (high + 1 - low)
                pairs = held.at[pl.ds(FULL + first, size)]
                copies.append(remote(stage.at[pl.ds(first, size)], pairs, send, ends, place.target(da, 0)))
        return copies

    order = arrival_order()
    for count, at in enumerate(order):
        rows = held.at[pl.ds(place.source(at) * RB, RB)]
        if at != (0, 0):
            remote(rows, rows, send, recv.at[slot_of(at)], here).wait_recv()
        for there in onward(at):
            remote(rows, rows, send, recv.at[slot_of(there)], place.target(there[0] - at[0], there[1] - at[1])).start()
        if between is not None:
            between(count)
        if count >= start:
            for old in waiting + [at]:
                for copy in pick(old):
                    copy.start()
            waiting = []
        else:
            waiting.append(at)
    for at in waiting:
        for copy in pick(at):
            copy.start()
    came = held.at[pl.ds(0, len(ROWS) * SIDE * CAP)]
    remote(came, came, send, ends, here).wait_recv()
    sent = held.at[pl.ds(0, (len(order) - 1) * RB + len(ROWS) * SIDE * CAP)]
    remote(sent, sent, send, ends, here).wait_send()


class ColGather:
    def __init__(self, place, own, rows, feat, send, recv, shift=0):
        self.place, self.own, self.rows, self.feat, self.send, self.recv = place, own, rows, feat, send, recv
        self.shift, self.size = shift, own.shape[0]

    def cut(self, x, core, part):
        start = (x % 4 * 2 + core) * self.feat
        if part is None:
            return self.rows.at[pl.ds(start + self.shift, self.size)]
        return self.rows.at[pl.ds(start + part * self.half, self.half)]

    def mine(self, part):
        if part is None:
            return self.own
        return self.own.at[pl.ds(part * self.half, self.half)]

    def begin(self):
        p = self.place
        for dx, sem in ((2, 2), (1, 0), (-1, 1)):
            remote(self.own, self.cut(p.x, p.core, None), self.send, self.recv.at[sem], p.beside(dx + 4, False)).start()
        remote(self.own, self.cut(p.x, p.core, None), self.send, self.recv.at[3], p.beside(0, True)).start()

    def wait(self, dx, other, sem):
        p = self.place
        core = 1 - p.core if other else p.core
        rows = self.cut(p.x + dx + 4, core, None)
        remote(rows, rows, self.send, self.recv.at[sem], (p.node, p.col)).wait_recv()
        return rows

    def forward(self, stage):
        p = self.place
        for dx, sem in ((-1, 0), (1, 1)) if stage == 0 else ((2, 2),):
            rows = self.wait(dx, False, sem)
            remote(rows, rows, self.send, self.recv.at[4 + sem], p.beside(0, True)).start()

    def finish(self):
        for dx, sem in ((0, 3), (-1, 4), (1, 5), (2, 6)):
            self.wait(dx, True, sem)
        sent = self.rows.at[pl.ds(0, 7 * self.size)]
        remote(sent, sent, self.send, self.recv.at[0], (self.place.node, self.place.col)).wait_send()


def tile_sum(index_ref, rows_ref, live, gathered, tiles, low, feat):
    total = tiles.shape[0]

    def step(g, acc):
        left, right = [], []
        for k in range(GROUP):
            t = g * GROUP + k
            block = gathered[index_ref[0, t], low : low + feat]
            row = jnp.where(t < live, rows_ref[t], RB)
            zero = jnp.zeros_like(block)
            left.append(jnp.concatenate([jnp.where(row == b, block, zero) for b in range(RB)], axis=0))
            right.append(tiles[t])
        return acc + lax.dot_general(
            jnp.concatenate(left, axis=1),
            jnp.concatenate(right, axis=1),
            (((1,), (1,)), ((), ())),
            preferred_element_type=jnp.float32,
        )

    return lax.fori_loop(0, total // GROUP, step, jnp.zeros((RB * feat, BLK), jnp.float32))


def as_column(row):
    size = row.shape[1]
    square = jnp.broadcast_to(row, (size, size))
    same = lax.broadcasted_iota(jnp.int32, (size, size), 0) == lax.broadcasted_iota(jnp.int32, (size, size), 1)
    return jnp.sum(jnp.where(same, square, 0.0), axis=1, keepdims=True)


def tile_plan(place, cols, live):
    total, nodes = cols.shape[1], SIDE * SIDE
    node, block = cols >> 2, cols & (RB - 1)
    alive = lax.broadcasted_iota(jnp.int32, (1, total), 1) < live
    node = jnp.where(alive, node, nodes)
    hit = lax.broadcasted_iota(jnp.int32, (nodes, total), 0) == node
    first = jnp.min(jnp.where(hit, block, RB - 1).astype(jnp.float32), axis=1, keepdims=True).astype(jnp.int32)
    last = jnp.max(jnp.where(hit, block, 0).astype(jnp.float32), axis=1, keepdims=True).astype(jnp.int32)
    lowest = jnp.min(jnp.where(hit, first, RB - 1).astype(jnp.float32), axis=0, keepdims=True).astype(jnp.int32)
    owner = cols >> 2
    u = (owner >> 3) * (1 - place.core) + (owner & (SIDE - 1)) * place.core
    a = (u - place.u + SIDE) & (SIDE - 1)
    line = (a == 0) | (a == 3) | (a == SIDE - 3)
    v = (owner & (SIDE - 1)) * (1 - place.core) + (owner >> 3) * place.core
    row = jnp.zeros_like(a)
    for i, at in enumerate(ROWS):
        row = jnp.where(a == at % SIDE, i, row)
    pair = (row * SIDE + ((place.v - v + NEAR) & (SIDE - 1))) * CAP
    beside = FULL + pair + jnp.where(block == lowest, 0, 1)
    return first, last, jnp.where(line, owner * RB + block, beside)


def kernel(
    colrow_ref, rows_ref, count_ref, x_ref, adj_ref, w1_ref, b1_ref, w2_ref, b2_ref, out_ref,
    held1, held2, tiles, w1_all, w2, b1_own, b1_all, y_own, y_all,
    stage, wanted, wanted_by, index_row, table, index_ref,
    recv1, recv2, col_recv, bias_recv, want_recv, sends, local,
):
    feat = y_own.shape[0]
    place = Place()
    fetch = [
        pltpu.make_async_copy(x_ref.at[:, pl.ds(k * BLK, BLK)], held1.at[place.node * RB + k], local.at[k]) for k in range(RB)
    ]
    fetch += [
        pltpu.make_async_copy(adj_ref, tiles, local.at[4]),
        pltpu.make_async_copy(w2_ref, w2, local.at[5]),
        pltpu.make_async_copy(w1_ref, w1_all.at[pl.ds(place.col * feat, feat)], local.at[6]),
    ]
    for copy in fetch:
        copy.start()

    barrier = pltpu.get_barrier_semaphore()
    greeted = [place.target(d, 0) for d in (1, -1, 3, -3)] + [place.target(0, d) for d in (1, -1, 2, -2)]
    greeted += [place.beside(dx, other) for dx in range(4) for other in (False, True) if dx or other]
    for device in greeted:
        pl.semaphore_signal(barrier, inc=1, device_id=device, device_id_type=MESH)
    for copy in fetch[:RB]:
        copy.wait()
    pl.semaphore_wait(barrier, len(greeted))

    asked = [remote(wanted, wanted_by.at[i], sends.at[5 + i], want_recv.at[i], place.target(d, 0)) for i, d in ((1, 1), (0, -1))]
    to_index = pltpu.make_async_copy(index_row, index_ref, local.at[7])
    to_table = pltpu.make_async_copy(wanted_by, table, local.at[8])

    weights = ColGather(place, w1_ref, w1_all, feat, sends.at[2], col_recv.at[0])
    peers = [(dx, other) for dx in range(4) for other in (False, True) if dx or other]

    def bias_copy(index, dx, other, coming):
        core = 1 - place.core if other else place.core
        x = (place.x - dx + 4) % 4 if coming else place.x
        source = x * 2 + (core if coming else place.core)
        rows = b1_all.at[pl.ds(source * feat, feat)]
        return remote(b1_own, rows, sends.at[4], bias_recv.at[index], place.beside(dx, other))

    def between(count):
        if count == 0:
            first, last, index = tile_plan(place, colrow_ref[...], count_ref[0])
            lane = lax.broadcasted_iota(jnp.int32, wanted.shape, 1)
            wanted[...] = jnp.where(lane == 0, first, last)
            index_row[:, 0 : index.shape[1]] = jnp.broadcast_to(index, (8, index.shape[1]))
            b1_own[...] = jnp.broadcast_to(as_column(b1_ref[...]), b1_own.shape)
            b1_all[pl.ds(place.col * feat, feat)] = b1_own[...]
            for copy in asked:
                copy.start()
            to_index.start()
            for index, (dx, other) in enumerate(peers):
                bias_copy(index, dx, other, False).start()
            weights.begin()
        elif count == TABLE:
            for copy in asked:
                copy.wait()
            to_table.start()
        elif count == TABLE + 1:
            to_table.wait()
        elif count == TABLE + 5:
            weights.forward(0)
        elif count == TABLE + 12:
            weights.forward(1)

    node_gather(place, held1, stage, table, sends.at[0], recv1, recv1.at[SLOTS], TABLE + 1, between)
    to_index.wait()
    weights.finish()
    for index, (dx, other) in enumerate(peers):
        bias_copy(index, dx, other, True).wait_recv()
    sent = b1_all.at[pl.ds(0, len(peers) * feat)]
    remote(sent, sent, sends.at[4], bias_recv.at[0], (place.node, place.col)).wait_send()
    for copy in fetch[RB:]:
        copy.wait()

    live = count_ref[0]
    exchanges = []
    part = feat // PARTS
    for p in range(PARTS):
        acc = tile_sum(index_ref, rows_ref, live, held1, tiles, p * part, part)
        for b in range(RB):
            y_own[p * part : (p + 1) * part, b * BLK : (b + 1) * BLK] = acc[b * part : (b + 1) * part].astype(y_own.dtype)
        y_all[pl.ds(place.col * feat + p * part, part)] = y_own[p * part : (p + 1) * part]
        own = y_own.at[pl.ds(p * part, part)]
        exchanges.append(ColGather(place, own, y_all, feat, sends.at[7 + p], col_recv.at[1 + p], p * part))
        exchanges[-1].begin()
    for leg in (0, 1):
        for exchange in exchanges:
            exchange.forward(leg)
    for exchange in exchanges:
        exchange.finish()

    wide = HALF * BLK
    step_rows = 128
    for n in range(RB // HALF):
        columns = pl.ds(n * wide, wide)
        total = jnp.zeros((feat, wide), jnp.float32)
        for m in range(w1_all.shape[0] // step_rows):
            span = pl.ds(m * step_rows, step_rows)
            z = jnp.dot(w1_all[span, :], y_all[:, columns], preferred_element_type=jnp.float32)
            bias = b1_all[span, :]
            h = jnp.maximum(z + jnp.concatenate([bias] * HALF, axis=1), 0.0).astype(jnp.bfloat16)
            total += jnp.dot(w2[:, span], h, preferred_element_type=jnp.float32)
        for k in range(HALF):
            held2[place.node * RB + n * HALF + k] = total[:, k * BLK : (k + 1) * BLK].astype(jnp.bfloat16)

    node_gather(place, held2, stage, table, sends.at[1], recv2, recv2.at[SLOTS])
    acc = tile_sum(index_ref, rows_ref, live, held2, tiles, 0, feat)
    bias = as_column(b2_ref[...])
    for b in range(RB):
        out_ref[:, b * BLK : (b + 1) * BLK] = acc[b * feat : (b + 1) * feat] + bias


def body(x_t, adj_tiles, tile_rows, tile_cols, tile_counts, w_first, b_first, w_second, b_second):
    feat, nodes = x_t.shape
    channels = w_first.shape[1]
    pairs = len(ROWS) * SIDE * CAP
    smem = pl.BlockSpec(memory_space=pltpu.SMEM)
    vmem = pl.BlockSpec(memory_space=pltpu.VMEM)
    hbm = pl.BlockSpec(memory_space=pl.ANY)
    dma = pltpu.SemaphoreType.DMA
    bf16 = jnp.bfloat16
    return pl.pallas_call(
        kernel,
        out_shape=jax.ShapeDtypeStruct((feat, nodes), jnp.float32),
        in_specs=[vmem, smem, smem, hbm, hbm, hbm, vmem, hbm, vmem],
        out_specs=vmem,
        scratch_shapes=[
            pltpu.VMEM((FULL + pairs, feat, BLK), bf16),
            pltpu.VMEM((FULL + pairs, feat, BLK), bf16),
            pltpu.VMEM(adj_tiles.shape, bf16),
            pltpu.VMEM((channels, channels), bf16),
            pltpu.VMEM((feat, channels), bf16),
            pltpu.VMEM((feat, BLK), jnp.float32),
            pltpu.VMEM((channels, BLK), jnp.float32),
            pltpu.VMEM((feat, nodes), bf16),
            pltpu.VMEM((channels, nodes), bf16),
            pltpu.VMEM((pairs, feat, BLK), bf16),
            pltpu.VMEM((SIDE * SIDE, BLK), jnp.int32),
            pltpu.VMEM((2, SIDE * SIDE, BLK), jnp.int32),
            pltpu.VMEM((8, BLK), jnp.int32),
            pltpu.SMEM((2, SIDE * SIDE, BLK), jnp.int32),
            pltpu.SMEM((8, BLK), jnp.int32),
            dma((SLOTS + 1,)),
            dma((SLOTS + 1,)),
            dma((1 + PARTS, 7)),
            dma((7,)),
            dma((2,)),
            dma((7 + PARTS,)),
            dma((9,)),
        ],
        compiler_params=pltpu.CompilerParams(collective_id=0, has_side_effects=True),
    )(tile_cols[None, :], tile_rows, tile_counts, x_t, adj_tiles, w_first, b_first[None, :], w_second, b_second[None, :])


def solution(mesh):
    return jax.shard_map(
        body,
        mesh=mesh,
        in_specs=(
            P("col", "node"),
            P("node", None, None),
            P("node"),
            P("node"),
            P("node"),
            P("col", None),
            P("col"),
            P("col", None),
            P("col"),
        ),
        out_specs=P("col", "node"),
        check_vma=False,
    )
```
